32 devices in a mesh: seg: 4 (over y, core), tm: 8 (over z, x).
Axes of the slice: x: 2, y: 2, z: 4, core: 2. Of those that a mesh axis runs over, the one named last changes fastest.
Arguments:
- transition: bfloat16 [64, 512, 512], P(('seg', 'tm')), may hold values from -1 to 1
- obs_gain: bfloat16 [64, 512, 512], P(('seg', 'tm')), may hold values from -0.0625 to 0.0625
- observed: bfloat16 [64, 4, 512], P(('seg', 'tm')), may hold values from -6 to 6
- init_mean: float32 [4, 512], replicated, may hold values from -6 to 6
- init_factor: float32 [512, 512], P('tm'), may hold values from -6 to 6
Outputs:
- means: float32 [64, 4, 512], P(('seg', 'tm'))
- factor_ends: float32 [4, 512, 512], P('seg', 'tm')
The draws below stay inside these ranges and needn't reach their ends.
All inputs are finite; a program needn't handle non-finite values.
Results may differ from the reference program's by a relative error of at most 0.0003.
Values sent between devices are 32-bit elements; how exact they have to be, the bound alone decides.
No kernel may reach another device: no remote copies, remote signals or barrier semaphores. Data moves between devices by JAX's collectives and lax.ppermute only.
A program may use at most 128 MiB of HBM per device.

```python
import jax
import jax.numpy as jnp
from jax import lax

D = 512
OBS = 512
SER = 4
STEPS_DEV = 2
TOTAL_TIME_STEPS = 64
N_SEG = 4
N_TM = 8


def draw_transition(key, part):
    random_keys = jax.random.split(key, 7)
    vectors = jax.random.normal(random_keys[0], (TOTAL_TIME_STEPS, D), jnp.float32)
    lengths = jnp.sum(vectors * vectors, axis=1)
    reflect = jnp.eye(D, dtype=jnp.float32)[None] - 2.0 * vectors[:, :, None] * vectors[:, None, :] / lengths[:, None, None]
    share = 0.5
    picker = jax.random.uniform(random_keys[1], (D,), jnp.float32)
    slow_rate = -jax.random.uniform(random_keys[2], (D,), jnp.float32, 0.2, 1.9) / TOTAL_TIME_STEPS
    fast_rate = -1.0 / jax.random.uniform(random_keys[3], (D,), jnp.float32, 30.0, 50.0)
    baseline_level = jnp.where(picker < share, slow_rate, fast_rate)
    random_perturbation = jax.random.uniform(random_keys[4], (TOTAL_TIME_STEPS, D), jnp.float32, 0.5, 1.5)
    spike_selector = jax.random.uniform(random_keys[5], (TOTAL_TIME_STEPS,), jnp.float32)
    spike_magnitude = jax.random.uniform(random_keys[6], (TOTAL_TIME_STEPS,), jnp.float32, 0.5, 0.8)
    spike_amount = jnp.where(spike_selector < 6.0 / TOTAL_TIME_STEPS, spike_magnitude, 1.0)
    noise_scale = jnp.exp(baseline_level[None, :] * random_perturbation) * spike_amount[:, None]
    return (reflect * noise_scale[:, None, :]).astype(jnp.bfloat16)


def level_of(stream_key, shape, shards, low, high):
    loudness, own = 1.0, jax.random.fold_in(stream_key, 6)
    for dim, blocks in shards:
        heights = jnp.exp(jax.random.uniform(jax.random.fold_in(own, dim), (blocks,), jnp.float32, low / len(shards), high / len(shards)))
        loudness = loudness * jnp.repeat(heights, shape[dim] // blocks).reshape([-1 if axis == dim else 1 for axis in range(len(shape))])
    return loudness


def gaussian(key, dims, spread, bound, pieces=(), held_as=jnp.bfloat16):
    level = level_of(key, dims, pieces, -0.22, 0.18) if pieces else 1.0
    values = jax.random.normal(key, dims, jnp.float32) * spread * level
    return jnp.minimum(jnp.maximum(values, -bound), bound).astype(held_as)


def setup_inputs(seed: int = 0) -> dict:
    key_of = jax.random.split(jax.random.key(seed), 6)
    return {
        "transition": draw_transition(jax.random.fold_in(key_of[5], 71), 0),
        "obs_gain": gaussian(key_of[1], (TOTAL_TIME_STEPS, OBS, D), (OBS * 16) ** -0.5, 0.0625, ((0, 32),)),
        "observed": gaussian(key_of[2], (TOTAL_TIME_STEPS, SER, OBS), 1.0, 6.0, ((0, 32),)),
        "init_mean": gaussian(key_of[3], (SER, D), 1.0, 6.0, (), jnp.float32),
        "init_factor": gaussian(key_of[4], (D, D), 1.0, 6.0, ((0, 8),), jnp.float32),
    }


def exact_dot(left, right):
    return jnp.dot(left, right, precision=lax.Precision.HIGHEST, preferred_element_type=jnp.float32)


def reference(transition, obs_gain, observed, init_mean, init_factor):
    per_block = STEPS_DEV * N_TM
    trans_blocks = transition.reshape(N_SEG, per_block, D, D)
    gain_blocks = obs_gain.reshape(N_SEG, per_block, OBS, D)
    seen_blocks = observed.reshape(N_SEG, per_block, SER, OBS)

    def inner(carry, inputs):
        mean_now, factor_now = carry
        matrix, gain, seen = inputs
        matrix = matrix.astype(jnp.float32)
        mean_now = exact_dot(mean_now, matrix) + jnp.dot(seen, gain, preferred_element_type=jnp.float32)
        factor_now = exact_dot(factor_now, matrix)
        return (mean_now, factor_now), mean_now

    def outer(carry, inputs):
        carry, block_means = lax.scan(inner, carry, inputs)
        return carry, (block_means, carry[1])

    start = (init_mean.astype(jnp.float32), init_factor.astype(jnp.float32))
    _, (all_means, ends) = lax.scan(outer, start, (trans_blocks, gain_blocks, seen_blocks))
    return all_means.reshape(TOTAL_TIME_STEPS, SER, D), ends
```

```python
import jax
import jax.numpy as jnp
from jax import lax
from jax.experimental import pallas as pl
from jax.experimental.pallas import tpu as pltpu
from jax.sharding import PartitionSpec as P

F32 = jnp.float32
BF16 = jnp.bfloat16
AXES = ("seg", "tm")


def halves(x):
    hi = x.astype(BF16)
    return hi, (x - hi.astype(F32)).astype(BF16)


def dot(a, b):
    return jnp.dot(a, b, preferred_element_type=F32)


def dot3(a_hi, a_lo, b_hi, b_lo):
    return dot(a_hi, b_hi) + (dot(a_hi, b_lo) + dot(a_lo, b_hi))


class Sizes:
    def __init__(self, width, series, chunks):
        self.width, self.series, self.chunks = width, series, chunks
        self.part = width // chunks
        self.tall = width + 16 * (-(-series // 16))
        self.buf = width + 8 * (-(-chunks * series // 8))
        self.low = self.tall - width


def put_rows(z, out, k, body, tail):
    for j in range(z.chunks):
        cols = slice(j * z.part, (j + 1) * z.part)
        out[j * z.part : (j + 1) * z.part, :] = body[:, cols]
        out[z.width + j * z.series : z.width + (j + 1) * z.series, :] = tail[:, cols]


def put_cols(z, out, k, body, tail):
    out[: z.width, :] = body
    out[z.width : z.width + z.series, :] = tail


def gather_rows(z, bufs, full):
    for k, buf in enumerate(bufs):
        for j in range(z.chunks):
            full[k * z.part : (k + 1) * z.part, j * z.part : (j + 1) * z.part] = buf[j * z.part : (j + 1) * z.part, :]
    for j in range(z.chunks):
        full[z.width : z.width + z.series, j * z.part : (j + 1) * z.part] = bufs[0][
            z.width + j * z.series : z.width + (j + 1) * z.series, :
        ]


def gather_cols(z, bufs, full):
    for k, buf in enumerate(bufs):
        cols = slice(k * z.part, (k + 1) * z.part)
        full[: z.width, cols] = buf[: z.width, :]
        full[z.width : z.width + z.series, cols] = buf[z.width : z.width + z.series, :]


def clear_low(z, full):
    full[z.width :, :] = jnp.zeros((z.low, z.width), F32)


def put_chunks(z, by_rows, outs, full):
    @pl.when(by_rows == 1)
    def _():
        for k, out in enumerate(outs):
            put_rows(z, out, k, full[k * z.part : (k + 1) * z.part, :], full[z.width : z.width + z.series, :])

    @pl.when(by_rows == 0)
    def _():
        for k, out in enumerate(outs):
            cols = slice(k * z.part, (k + 1) * z.part)
            put_cols(z, out, k, full[: z.width, cols], full[z.width : z.width + z.series, cols])


def call(kernel, outs, operands, flags=None, scratch=(), name=None):
    in_specs = [pl.BlockSpec(memory_space=pltpu.VMEM) for _ in operands]
    if flags is not None:
        in_specs = [pl.BlockSpec(memory_space=pltpu.SMEM)] + in_specs
        operands = [flags] + list(operands)
    return pl.pallas_call(
        kernel,
        out_shape=outs,
        in_specs=in_specs,
        out_specs=jax.tree.map(lambda _: pl.BlockSpec(memory_space=pltpu.VMEM), outs),
        scratch_shapes=list(scratch),
        name=name,
    )(*operands)


def shape(rows, cols, dtype=F32):
    return jax.ShapeDtypeStruct((rows, cols), dtype)


def local_map(z, flags, transition, gain, observed):
    steps = transition.shape[0]

    def kernel(flag, t, g, o, *rest):
        chunks, (whole, hi, lo, tail, drive) = rest[: z.chunks], rest[z.chunks :]
        drives = [dot(o[i], g[i]) for i in range(steps)]
        for i in range(steps):
            drive[i] = drives[i]
        body, low = t[0], drives[0]
        for i in range(1, steps):
            if i == 1:
                body = dot(body, t[i])
            else:
                b_hi, b_lo = halves(body)
                body = dot(b_hi, t[i]) + dot(b_lo, t[i])
            l_hi, l_lo = halves(low)
            low = dot(l_hi, t[i]) + dot(l_lo, t[i]) + drives[i]
        clear_low(z, whole)
        whole[: z.width, :] = body.astype(F32)
        whole[z.width : z.width + z.series, :] = low
        tail[...] = low
        put_chunks(z, flag[0], chunks, whole)
        hi[...], lo[...] = halves(whole[...])

    outs = [shape(z.buf, z.part)] * z.chunks + [
        shape(z.tall, z.width),
        shape(z.tall, z.width, BF16),
        shape(z.tall, z.width, BF16),
        shape(z.series, z.width),
        jax.ShapeDtypeStruct((steps, z.series, z.width), F32),
    ]
    res = call(kernel, outs, [transition, gain, observed], flags, name="local_map")
    return (res[: z.chunks], *res[z.chunks :])


def times_chunk(z, flags, chunk, hi, lo, tail):
    def kernel(flag, got, own_hi, own_lo, own_tail, out, left):
        @pl.when(flag[0] == 1)
        def _():
            left[z.part :, :] = jnp.zeros((left.shape[0] - z.part, z.width), F32)
            for j in range(z.chunks):
                cols = slice(j * z.part, (j + 1) * z.part)
                left[: z.part, cols] = got[j * z.part : (j + 1) * z.part, :]
                left[z.part : z.part + z.series, cols] = got[z.width + j * z.series : z.width + (j + 1) * z.series, :]
            l_hi, l_lo = halves(left[...])
            res = dot3(l_hi, l_lo, own_hi[: z.width, :], own_lo[: z.width, :])
            put_rows(z, out, 0, res[: z.part], res[z.part : z.part + z.series] + own_tail[...])

        @pl.when(flag[0] == 0)
        def _():
            r_hi, r_lo = halves(got[: z.width, :])
            res = dot3(own_hi[...], own_lo[...], r_hi, r_lo)
            out[z.width :, :] = jnp.zeros((z.buf - z.width, z.part), F32)
            put_cols(z, out, 0, res[: z.width], res[z.width : z.width + z.series] + got[z.width : z.width + z.series, :])

    return call(
        kernel,
        shape(z.buf, z.part),
        [chunk, hi, lo, tail],
        flags,
        scratch=[pltpu.VMEM((z.part + z.low, z.width), F32)],
        name="times_chunk",
    )


def merge(z, flags, got, own):
    def kernel(flag, *refs):
        n = z.chunks
        gots, owns = refs[:n], refs[n : 2 * n]
        outs = refs[2 * n : 3 * n]
        hi, lo, tail, left_hi, left_lo, left_tail = refs[3 * n : 3 * n + 6]
        a, b, c = refs[3 * n + 6 :]
        clear_low(z, a)
        clear_low(z, b)

        def load(first, second):
            @pl.when(flag[0] == 1)
            def _():
                gather_rows(z, first, a)
                gather_rows(z, second, b)

            @pl.when(flag[0] == 0)
            def _():
                gather_cols(z, first, a)
                gather_cols(z, second, b)

        @pl.when(flag[1] == 1)
        def _():
            load(gots, owns)

        @pl.when(flag[1] == 0)
        def _():
            load(owns, gots)

        left_hi[...], left_lo[...] = halves(a[...])
        left_tail[...] = a[z.width : z.width + z.series, :]
        r_hi, r_lo = halves(b[: z.width, :])
        c[...] = dot3(left_hi[...], left_lo[...], r_hi, r_lo)
        c[z.width : z.width + z.series, :] = c[z.width : z.width + z.series, :] + b[z.width : z.width + z.series, :]
        put_chunks(z, flag[2], outs, c)
        hi[...], lo[...] = halves(c[...])
        tail[...] = c[z.width : z.width + z.series, :]

    pair = [shape(z.tall, z.width, BF16), shape(z.tall, z.width, BF16), shape(z.series, z.width)]
    res = call(
        kernel,
        [shape(z.buf, z.part)] * z.chunks + pair + pair,
        list(got) + list(own),
        flags,
        scratch=[pltpu.VMEM((z.tall, z.width), F32)] * 3,
        name="merge",
    )
    n = z.chunks
    return res[:n], tuple(res[n : n + 3]), tuple(res[n + 3 :])


def assemble(z, flags, chunks):
    def kernel(flag, *refs):
        bufs, (hi, lo, tail, full) = refs[: z.chunks], refs[z.chunks :]
        clear_low(z, full)

        @pl.when(flag[0] == 1)
        def _():
            gather_rows(z, bufs, full)

        @pl.when(flag[0] == 0)
        def _():
            gather_cols(z, bufs, full)

        hi[...], lo[...] = halves(full[...])
        tail[...] = full[z.width : z.width + z.series, :]

    return call(
        kernel,
        [shape(z.tall, z.width, BF16), shape(z.tall, z.width, BF16), shape(z.series, z.width)],
        chunks,
        flags,
        scratch=[pltpu.VMEM((z.tall, z.width), F32)],
        name="assemble",
    )


def advance(z, state, rows, mapped):
    def kernel(s, hi, lo, tail, out):
        s_hi, s_lo = halves(s[...])
        out[...] = dot3(s_hi, s_lo, hi[: z.width, :], lo[: z.width, :])
        out[rows : rows + z.series, :] = out[rows : rows + z.series, :] + tail[...]

    return call(kernel, shape(*state.shape), [state, *mapped], name="advance")


def last_steps(z, flags, entry, first, back, transition, drive):
    steps = transition.shape[0]

    def kernel(flag, e, *refs):
        bufs, (given, t, d, out, full, now) = refs[: z.chunks], refs[z.chunks :]
        now[...] = e[...]

        @pl.when(flag[0] == 1)
        def _():
            @pl.when(flag[1] == 1)
            def _():
                gather_rows(z, bufs, full)

            @pl.when(flag[1] == 0)
            def _():
                full[: z.width + z.series, :] = given[: z.width + z.series, :]

            e_hi, e_lo = halves(e[...])
            hi, lo = halves(full[: z.width, :])
            now[...] = dot3(e_hi, e_lo, hi, lo)
            now[: z.series, :] = now[: z.series, :] + full[z.width : z.width + z.series, :]

        for i in range(steps):
            n_hi, n_lo = halves(now[...])
            now[...] = dot(n_hi, t[i]) + dot(n_lo, t[i])
            now[: z.series, :] = now[: z.series, :] + d[i]
            out[i] = now[: z.series, :]

    return call(
        kernel,
        jax.ShapeDtypeStruct((steps, z.series, z.width), F32),
        [entry, *first, back, transition, drive],
        flags,
        scratch=[pltpu.VMEM((z.tall, z.width), F32), pltpu.VMEM(entry.shape, F32)],
        name="last_steps",
    )


class Tree:
    def __init__(self, segs, size):
        self.segs, self.size = segs, size
        self.depth = size.bit_length() - 1
        if size != 1 << self.depth or self.depth < 3:
            raise ValueError("tm size")

    def root(self, odd, level, group):
        if level == 1:
            return 2 * group + (0 if odd else 1)
        return self.root(odd, level - 1, 2 * group + (1 - group % 2))

    def pairs(self, per_parity):
        return [
            (s * self.size + a, s * self.size + b) for s in range(self.segs) for a, b in per_parity(s % 2)
        ]

    def child_roots(self, odd, level, group):
        return self.root(odd, level - 1, 2 * group), self.root(odd, level - 1, 2 * group + 1)

    def up(self, level):
        def of(odd):
            if level == 1:
                return [(i, i ^ 1) for i in range(self.size) if i % 2 == (1 if odd else 0)]
            found = []
            for g in range(self.size >> level):
                a, b = self.child_roots(odd, level, g)
                if level == self.depth:
                    found += [(a, b), (b, a)]
                else:
                    found.append((a, b) if g % 2 == 0 else (b, a))
            return found

        return self.pairs(of)

    def spread(self):
        stages = []
        holders = {odd: set(self.child_roots(odd, self.depth, 0)) for odd in (0, 1)}
        bit = self.size // 4
        while bit:
            now = {odd: sorted(holders[odd]) for odd in (0, 1)}
            stages.append((bit, self.pairs(lambda odd: [(i, i ^ bit) for i in now[odd]])))
            for odd in (0, 1):
                holders[odd] |= {i ^ bit for i in now[odd]}
            bit //= 2
        return stages

    def is_in(self, pairs, which):
        hit = [0] * (self.segs * self.size)
        for pair in pairs:
            hit[pair[which]] = 1
        return hit


def make(mesh):
    segs, size = mesh.shape["seg"], mesh.shape["tm"]
    tree = Tree(segs, size)
    depth = tree.depth

    def send(x, pairs):
        return lax.ppermute(x, AXES, pairs)

    def per_device(transition, obs_gain, observed, init_mean, init_factor):
        width, series = transition.shape[1], observed.shape[1]
        chunks = next(n for n in (4, 2, 1) if width % (n * 128) == 0 or n == 1)
        z = Sizes(width, series, chunks)
        seg, tm = lax.axis_index("seg"), lax.axis_index("tm")
        me = seg * size + tm
        even = (1 - seg % 2).astype(jnp.int32)
        right_half = (tm >= size // 2).astype(jnp.int32)

        def member(table):
            return jnp.asarray(table, jnp.int32)[me]

        def flags(*values):
            return jnp.stack([jnp.asarray(v, jnp.int32) for v in values])

        own, whole, hi, lo, tail, drive = local_map(z, flags(even), transition, obs_gain, observed)
        first = [send(c, tree.up(1)) for c in own]
        pair_flag = flags(even)
        outs = [times_chunk(z, pair_flag, c, hi, lo, tail) for c in first]
        lefts = {}
        by_rows = even
        for level in range(2, depth):
            got = [send(c, tree.up(level)) for c in outs]
            side = 1 - (tm >> level) % 2
            next_rows = 1 - right_half if level == depth - 1 else jnp.int32(1)
            outs, mine, lefts[level] = merge(z, flags(by_rows, side, next_rows), got, outs)
            by_rows = next_rows
        crossed = [send(c, tree.up(depth)) for c in outs]
        back = send(whole, tree.pairs(lambda odd: [(i, i + 1) for i in range(0, size, 2)] if odd else []))
        final = [times_chunk(z, flags(right_half), c, *mine) for c in crossed]
        for bit, pairs in tree.spread():
            new = member(tree.is_in(pairs, 1)) == 1
            final = [jnp.where(new, send(c, pairs), c) for c in final]
        block = assemble(z, flags(right_half), final)

        rows = init_factor.shape[0]
        low = 8 * (-(-series // 8))
        state = jnp.concatenate([init_factor, init_mean, jnp.zeros((low - series, width), F32)])
        for turn in range(segs - 1):
            moved = advance(z, state, rows, block)
            arrived = send(moved, [(turn * size + i, (turn + 1) * size + i) for i in range(size)])
            state = jnp.where(seg == turn + 1, arrived, state)
        ends = advance(z, state, rows, block)[:rows]

        entry = state[rows:]
        halfway = assemble(z, flags(1), crossed)
        entry = jnp.where(right_half == 1, advance(z, entry, 0, halfway), entry)
        for level in range(depth - 1, 1, -1):
            beyond = advance(z, entry, 0, lefts[level])
            right_sub = (tm >> level) % 2 == 0
            mine_in = jnp.where(right_sub, beyond, entry)
            other_in = jnp.where(right_sub, entry, beyond)

            def others(odd, final):
                found = []
                for g in range(size >> level):
                    root = tree.root(odd, level, g)
                    a, b = tree.child_roots(odd, level, g)
                    found.append((root, (a if root == b else b) ^ final))
                return found

            cross = tree.pairs(lambda odd: others(odd, 0))
            got = send(other_in, cross)
            entry = jnp.where(member(tree.is_in(cross, 1)) == 1, got, mine_in)
            if level == 2:
                cross = tree.pairs(lambda odd: others(odd, 1))
                got = send(other_in, cross)
                entry = jnp.where(member(tree.is_in(cross, 1)) == 1, got, entry)
                near = tree.pairs(lambda odd: [(tree.root(odd, 2, g), tree.root(odd, 2, g) ^ 1) for g in range(size >> 2)])
                got = send(mine_in, near)
                entry = jnp.where(member(tree.is_in(near, 1)) == 1, got, entry)
        means = last_steps(z, flags(tm % 2, even), entry, first, back, transition, drive)
        return means, ends[None]

    return per_device


def solution(mesh):
    return jax.shard_map(
        make(mesh),
        mesh=mesh,
        in_specs=(
            P(("seg", "tm"), None, None),
            P(("seg", "tm"), None, None),
            P(("seg", "tm"), None, None),
            P(),
            P("tm", None),
        ),
        out_specs=(P(("seg", "tm"), None, None), P("seg", "tm", None)),
        check_vma=False,
    )
```

```python
import jax
import jax.numpy as jnp
from jax import lax
from jax.experimental import pallas as pl
from jax.experimental.pallas import tpu as pltpu
from jax.sharding import PartitionSpec as P

F32 = jnp.float32
BF16 = jnp.bfloat16
AXES = ("seg", "tm")
GRANT = 10 * 1024 * 1024
AHEAD = 2


def halves(x):
    hi = x.astype(BF16)
    return hi, (x - hi.astype(F32)).astype(BF16)


def dot(a, b):
    return jnp.dot(a, b, preferred_element_type=F32)


def dot3(a_hi, a_lo, b_hi, b_lo):
    return dot(a_hi, b_hi) + (dot(a_hi, b_lo) + dot(a_lo, b_hi))


def few(rows, hi, lo=None):
    r_hi = rows.astype(BF16)
    r_hi32 = r_hi.astype(F32)
    both = jnp.concatenate([r_hi32, rows - r_hi32]).astype(BF16)
    res = dot(both, hi)
    res = res[: rows.shape[0]] + res[rows.shape[0] :]
    return res if lo is None else res + dot(r_hi, lo)


class Sizes:
    def __init__(self, width, series, chunks):
        self.width, self.series, self.chunks = width, series, chunks
        self.part = width // chunks
        self.tall = width + 16 * (-(-series // 16))
        self.buf = width + 8 * (-(-chunks * series // 8))
        self.low = self.tall - width


def put_rows(z, out, k, body, tail):
    for j in range(z.chunks):
        cols = slice(j * z.part, (j + 1) * z.part)
        out[j * z.part : (j + 1) * z.part, :] = body[:, cols]
        out[z.width + j * z.series : z.width + (j + 1) * z.series, :] = tail[:, cols]


def put_cols(z, out, k, body, tail):
    out[: z.width, :] = body
    out[z.width : z.width + z.series, :] = tail


def gather_rows(z, bufs, full):
    for k, buf in enumerate(bufs):
        for j in range(z.chunks):
            full[k * z.part : (k + 1) * z.part, j * z.part : (j + 1) * z.part] = buf[j * z.part : (j + 1) * z.part, :]
    for j in range(z.chunks):
        full[z.width : z.width + z.series, j * z.part : (j + 1) * z.part] = bufs[0][
            z.width + j * z.series : z.width + (j + 1) * z.series, :
        ]


def gather_cols(z, bufs, full):
    for k, buf in enumerate(bufs):
        cols = slice(k * z.part, (k + 1) * z.part)
        full[: z.width, cols] = buf[: z.width, :]
        full[z.width : z.width + z.series, cols] = buf[z.width : z.width + z.series, :]


def clear_low(z, full):
    full[z.width :, :] = jnp.zeros((z.low, z.width), F32)


def put_chunks(z, by_rows, outs, full):
    @pl.when(by_rows)
    def _():
        for k, out in enumerate(outs):
            put_rows(z, out, k, full[k * z.part : (k + 1) * z.part, :], full[z.width : z.width + z.series, :])

    @pl.when(jnp.logical_not(by_rows))
    def _():
        for k, out in enumerate(outs):
            cols = slice(k * z.part, (k + 1) * z.part)
            put_cols(z, out, k, full[: z.width, cols], full[z.width : z.width + z.series, cols])


def call(kernel, outs, operands, where=None, scratch=(), name=None, far=0):
    in_specs = [pl.BlockSpec(memory_space=pltpu.HBM if i < far else pltpu.VMEM) for i in range(len(operands))]
    operands = [pltpu.with_memory_space_constraint(x, pltpu.HBM) if i < far else x for i, x in enumerate(operands)]

    def body(*refs):
        if where is None:
            kernel(*refs)
        else:
            kernel(where(lax.axis_index("seg"), lax.axis_index("tm")), *refs)

    return pl.pallas_call(
        body,
        out_shape=outs,
        in_specs=in_specs,
        out_specs=jax.tree.map(lambda _: pl.BlockSpec(memory_space=pltpu.VMEM), outs),
        scratch_shapes=list(scratch),
        compiler_params=pltpu.CompilerParams(vmem_limit_bytes=GRANT),
        name=name,
    )(*operands)


def shape(rows, cols, dtype=F32):
    return jax.ShapeDtypeStruct((rows, cols), dtype)


def gather(z, by_rows, bufs, full):
    @pl.when(by_rows)
    def _():
        gather_rows(z, bufs, full)

    @pl.when(jnp.logical_not(by_rows))
    def _():
        gather_cols(z, bufs, full)


def map_shapes(z):
    return [shape(z.tall, z.width, BF16), shape(z.tall, z.width, BF16), shape(z.series, z.width)]


def local_map(z, where, transition, gain, observed):
    steps = transition.shape[0]

    def kernel(by_rows, t_hbm, g_hbm, o, *rest):
        chunks, (whole, hi, lo, tail, drive) = rest[: z.chunks], rest[z.chunks : z.chunks + 5]
        t, g, sems = rest[z.chunks + 5 :]
        copies = [
            pltpu.make_async_copy(t_hbm, t, sems.at[0]),
            pltpu.make_async_copy(g_hbm, g, sems.at[1]),
        ]
        for copy in copies:
            copy.start()
        copies[0].wait()
        body = t[0]
        for i in range(1, steps):
            if i == 1:
                body = dot(body, t[i])
            else:
                b_hi, b_lo = halves(body)
                body = dot(b_hi, t[i]) + dot(b_lo, t[i])
        clear_low(z, whole)
        whole[: z.width, :] = body.astype(F32)
        copies[1].wait()
        drives = [dot(o[i], g[i]) for i in range(steps)]
        low = drives[0]
        for i in range(steps):
            drive[i] = drives[i]
            if i:
                l_hi, l_lo = halves(low)
                low = dot(l_hi, t[i]) + dot(l_lo, t[i]) + drives[i]
        whole[z.width : z.width + z.series, :] = low
        tail[...] = low
        put_chunks(z, by_rows, chunks, whole)
        hi[...], lo[...] = halves(whole[...])

    res = call(
        kernel,
        [shape(z.buf, z.part)] * z.chunks
        + [shape(z.tall, z.width)]
        + map_shapes(z)
        + [jax.ShapeDtypeStruct((steps, z.series, z.width), F32)],
        [transition, gain, observed],
        where,
        scratch=[
            pltpu.VMEM(transition.shape, transition.dtype),
            pltpu.VMEM(gain.shape, gain.dtype),
            pltpu.SemaphoreType.DMA((2,)),
        ],
        name="local_map",
        far=2,
    )
    n = z.chunks
    return res[:n], res[n], tuple(res[n + 1 : n + 4]), res[n + 4]


def times_chunk(z, where, chunk, own):
    def kernel(by_rows, got, own_hi, own_lo, own_tail, out, left):
        @pl.when(by_rows)
        def _():
            left[z.part :, :] = jnp.zeros((left.shape[0] - z.part, z.width), F32)
            for j in range(z.chunks):
                cols = slice(j * z.part, (j + 1) * z.part)
                left[: z.part, cols] = got[j * z.part : (j + 1) * z.part, :]
                left[z.part : z.part + z.series, cols] = got[z.width + j * z.series : z.width + (j + 1) * z.series, :]
            l_hi, l_lo = halves(left[...])
            res = dot3(l_hi, l_lo, own_hi[: z.width, :], own_lo[: z.width, :])
            put_rows(z, out, 0, res[: z.part], res[z.part : z.part + z.series] + own_tail[...])

        @pl.when(jnp.logical_not(by_rows))
        def _():
            r_hi, r_lo = halves(got[: z.width, :])
            res = dot3(own_hi[...], own_lo[...], r_hi, r_lo)
            out[z.width :, :] = jnp.zeros((z.buf - z.width, z.part), F32)
            put_cols(z, out, 0, res[: z.width], res[z.width : z.width + z.series] + got[z.width : z.width + z.series, :])

    return call(
        kernel,
        shape(z.buf, z.part),
        [chunk, *own],
        where,
        scratch=[pltpu.VMEM((z.part + z.low, z.width), F32)],
        name="times_chunk",
    )


def merge(z, where, got, own):
    def kernel(flag, *refs):
        by_rows, got_left, next_rows = flag
        n = z.chunks
        gots, owns = refs[:n], refs[n : 2 * n]
        outs = refs[2 * n : 3 * n]
        hi, lo, tail, left_hi, left_lo, left_tail = refs[3 * n : 3 * n + 6]
        a, b, c = refs[3 * n + 6 :]
        clear_low(z, a)
        clear_low(z, b)

        @pl.when(got_left)
        def _():
            gather(z, by_rows, gots, a)
            gather(z, by_rows, owns, b)

        @pl.when(jnp.logical_not(got_left))
        def _():
            gather(z, by_rows, owns, a)
            gather(z, by_rows, gots, b)

        left_hi[...], left_lo[...] = halves(a[...])
        left_tail[...] = a[z.width : z.width + z.series, :]
        r_hi, r_lo = halves(b[: z.width, :])
        c[...] = dot3(left_hi[...], left_lo[...], r_hi, r_lo)
        c[z.width : z.width + z.series, :] = c[z.width : z.width + z.series, :] + b[z.width : z.width + z.series, :]
        put_chunks(z, next_rows, outs, c)
        hi[...], lo[...] = halves(c[...])
        tail[...] = c[z.width : z.width + z.series, :]

    res = call(
        kernel,
        [shape(z.buf, z.part)] * z.chunks + map_shapes(z) * 2,
        list(got) + list(own),
        where,
        scratch=[pltpu.VMEM((z.tall, z.width), F32)] * 3,
        name="merge",
    )
    n = z.chunks
    return res[:n], tuple(res[n : n + 3]), tuple(res[n + 3 :])


def pick(z, where, got, own):
    def kernel(new, a, b, out):
        @pl.when(new)
        def _():
            out[...] = a[...]

        @pl.when(jnp.logical_not(new))
        def _():
            out[...] = b[...]

    return call(kernel, shape(z.buf, z.part), [got, own], where, name="pick")


def assemble(z, where, chunks, others=None):
    extra = [] if others is None else list(others)

    def kernel(flag, *refs):
        by_rows, swap = flag
        n = z.chunks
        bufs, rest = refs[:n], refs[n : n + len(extra)]
        hi, lo, tail, full = refs[n + len(extra) :]
        clear_low(z, full)
        if not extra:
            gather(z, by_rows, bufs, full)
        else:

            @pl.when(jnp.logical_not(swap))
            def _():
                gather(z, by_rows, bufs, full)

            @pl.when(swap)
            def _():
                if len(rest) == 1:
                    full[...] = rest[0][...]
                else:
                    gather(z, by_rows, rest, full)

        hi[...], lo[...] = halves(full[...])
        tail[...] = full[z.width : z.width + z.series, :]

    return call(
        kernel,
        map_shapes(z),
        list(chunks) + extra,
        where,
        scratch=[pltpu.VMEM((z.tall, z.width), F32)],
        name="assemble",
    )


def padded(series):
    return 8 * (-(-series // 8))


def advance(z, state, block):
    first = isinstance(state, tuple)
    parts = list(state) if first else [state]
    rows = parts[0].shape[0] - (0 if first else padded(z.series))

    def kernel(*refs):
        given, (hi, lo, tail, out) = refs[: len(parts)], refs[len(parts) :]
        if first:
            out[rows:, :] = jnp.zeros((out.shape[0] - rows, z.width), F32)
            out[:rows, :] = given[0][...]
            out[rows : rows + z.series, :] = given[1][...]
            now = out[...]
        else:
            now = given[0][...]
        out[...] = few(now, hi[: z.width, :], lo[: z.width, :])
        out[rows : rows + z.series, :] = out[rows : rows + z.series, :] + tail[...]

    return call(kernel, shape(rows + padded(z.series), z.width), [*parts, *block], name="advance")


def chosen(z, where, moved):
    rows = moved[0].shape[0] - padded(z.series)

    def kernel(seg, *refs):
        out = refs[-1]
        for i, ref in enumerate(refs[:-1]):

            @pl.when(seg == i)
            def _():
                out[0] = ref[:rows, :]

    return call(
        kernel, jax.ShapeDtypeStruct((1, rows, z.width), F32), list(moved), where, name="chosen"
    )


def load_choice(z, index, refs, into):
    for i, ref in enumerate(refs):

        @pl.when(index == i)
        def _():
            if ref.shape[0] == z.series:
                into[...] = jnp.zeros(into.shape, F32)
                into[: z.series, :] = ref[...]
            else:
                into[...] = ref[ref.shape[0] - into.shape[0] :, :]


def descend(z, where, candidates, left, cross=None):
    low = padded(z.series)
    m = len(candidates)
    maps = list(left) + ([] if cross is None else list(cross))

    def kernel(flag, *refs):
        index, through, in_right = flag
        hi, lo, tail = refs[m : m + 3]
        mine, other, now = refs[m + len(maps) :]
        load_choice(z, index, refs[:m], now)
        if cross is not None:

            @pl.when(through)
            def _():
                c_hi, c_lo, c_tail = refs[m + 3 : m + 6]
                now[...] = few(now[...], c_hi[: z.width, :], c_lo[: z.width, :])
                now[: z.series, :] = now[: z.series, :] + c_tail[...]

        beyond = few(now[...], hi[: z.width, :], lo[: z.width, :])

        @pl.when(in_right)
        def _():
            mine[...] = beyond
            mine[: z.series, :] = mine[: z.series, :] + tail[...]
            other[...] = now[...]

        @pl.when(jnp.logical_not(in_right))
        def _():
            other[...] = beyond
            other[: z.series, :] = other[: z.series, :] + tail[...]
            mine[...] = now[...]

    return call(
        kernel,
        [shape(low, z.width)] * 2,
        [*candidates, *maps],
        where,
        scratch=[pltpu.VMEM((low, z.width), F32)],
        name="descend",
    )


def last_steps(z, where, candidates, left, transition, drive):
    steps = transition.shape[0]
    m = len(candidates)
    low = padded(z.series)

    def kernel(flag, *refs):
        index, through = flag
        hi, lo, tail, t, d, out, now = refs[m:]
        load_choice(z, index, refs[:m], now)

        @pl.when(through)
        def _():
            now[...] = few(now[...], hi[: z.width, :], lo[: z.width, :])
            now[: z.series, :] = now[: z.series, :] + tail[...]

        for i in range(steps):
            now[...] = few(now[...], t[i])
            now[: z.series, :] = now[: z.series, :] + d[i]
            out[i] = now[: z.series, :]

    return call(
        kernel,
        jax.ShapeDtypeStruct((steps, z.series, z.width), F32),
        [*candidates, *left, transition, drive],
        where,
        scratch=[pltpu.VMEM((low, z.width), F32)],
        name="last_steps",
    )


class Tree:
    def __init__(self, segs, size):
        self.segs, self.size = segs, size
        self.depth = size.bit_length() - 1
        if size != 1 << self.depth or self.depth < 3:
            raise ValueError("tm size")

    def root(self, odd, level, group):
        if level == 1:
            return 2 * group + (0 if odd else 1)
        return self.root(odd, level - 1, 2 * group + (1 - group % 2))

    def pairs(self, per_parity):
        return [
            (s * self.size + a, s * self.size + b) for s in range(self.segs) for a, b in per_parity(s % 2)
        ]

    def child_roots(self, odd, level, group):
        return self.root(odd, level - 1, 2 * group), self.root(odd, level - 1, 2 * group + 1)

    def up(self, level):
        def of(odd):
            if level == 1:
                return [(i, i ^ 1) for i in range(self.size) if i % 2 == (1 if odd else 0)]
            found = []
            for g in range(self.size >> level):
                a, b = self.child_roots(odd, level, g)
                if level == self.depth:
                    found += [(a, b), (b, a)]
                else:
                    found.append((a, b) if g % 2 == 0 else (b, a))
            return found

        return self.pairs(of)

    def spread(self):
        stages = []
        holders = {odd: set(self.child_roots(odd, self.depth, 0)) for odd in (0, 1)}
        bit = self.size // 4
        while bit:
            now = {odd: sorted(holders[odd]) for odd in (0, 1)}
            stages.append((bit, self.pairs(lambda odd: [(i, i ^ bit) for i in now[odd]])))
            for odd in (0, 1):
                holders[odd] |= {i ^ bit for i in now[odd]}
            bit //= 2
        return stages

    def root_of(self, odd, level, group):
        for _ in range(level - 1):
            group = 2 * group + 1 - group % 2
        return 2 * group + 1 - odd


def tied(x, after):
    return lax.optimization_barrier((x, after))[0]


def make(mesh):
    segs, size = mesh.shape["seg"], mesh.shape["tm"]
    tree = Tree(segs, size)
    depth = tree.depth
    half = size // 2

    def send(x, pairs):
        return lax.ppermute(x, AXES, pairs)

    def others(level, flip):
        def of(odd):
            found = []
            for g in range(size >> level):
                root = tree.root(odd, level, g)
                a, b = tree.child_roots(odd, level, g)
                found.append((root, (a if root == b else b) ^ flip))
            return found

        return tree.pairs(of)

    def top_and_other(seg, tm, level):
        odd, group = seg % 2, tm >> level
        top = tree.root_of(odd, level, group)
        a, b = (tree.root_of(odd, level - 1, 2 * group + i) for i in (0, 1))
        return top, a + b - top

    def per_device(transition, obs_gain, observed, init_mean, init_factor):
        width, series = transition.shape[1], observed.shape[1]
        chunks = next(n for n in (4, 2, 1) if width % (n * 128) == 0 or n == 1)
        z = Sizes(width, series, chunks)

        def is_even(seg, tm):
            return seg % 2 == 0

        def in_right_half(seg, tm):
            return tm >= half

        own, whole, own_map, drive = local_map(z, is_even, transition, obs_gain, observed)
        first = [send(c, tree.up(1)) for c in own]
        outs = [times_chunk(z, is_even, c, own_map) for c in first]
        back = send(
            tied(whole, outs[-1]), tree.pairs(lambda odd: [(i, i + 1) for i in range(0, size, 2)] if odd else [])
        )
        lefts = {}
        for level in range(2, depth):

            def where(seg, tm, level=level):
                by_rows = seg % 2 == 0 if level == 2 else seg >= 0
                next_rows = tm < half if level == depth - 1 else seg >= 0
                return by_rows, (tm >> level) % 2 == 0, next_rows

            got = [send(c, tree.up(level)) for c in outs]
            outs, mine, lefts[level] = merge(z, where, got, outs)
        crossed, final = [], []
        for k, c in enumerate(outs):
            crossed.append(send(c if k < AHEAD else tied(c, final[k - AHEAD]), tree.up(depth)))
            final.append(times_chunk(z, in_right_half, crossed[k], mine))
        left = assemble(z, lambda seg, tm: (seg >= 0, seg % 2 == 1), first, [back])
        final[-1], left = lax.optimization_barrier((final[-1], left))

        stages = tree.spread()
        for bit, pairs in stages:

            def new(seg, tm, bit=bit):
                away = tm ^ tree.root_of(seg % 2, depth - 1, tm // half)
                return away & (2 * bit - 1) == bit

            got = [send(c, pairs) for c in final]
            if bit > 1:
                final = [pick(z, new, g, c) for g, c in zip(got, final)]
        block = assemble(z, lambda seg, tm: (tm >= half, new(seg, tm)), final, got)

        arrived, moved = [], [advance(z, (init_factor, init_mean), block)]
        for turn in range(segs - 1):
            arrived.append(send(moved[-1], [(turn * size + i, (turn + 1) * size + i) for i in range(size)]))
            moved.append(advance(z, arrived[-1], block))
        ends = chosen(z, lambda seg, tm: seg, moved)

        halfway = assemble(z, lambda seg, tm: (seg >= 0, seg < 0), crossed)
        candidates, cross = [init_mean, *arrived], halfway
        for level in range(depth - 1, 1, -1):

            def where(seg, tm, level=level):
                if level == depth - 1:
                    index = seg
                else:
                    index = (tm == top_and_other(seg, tm, level + 1)[1]).astype(jnp.int32)
                return index, tm >= half, (tm >> level) % 2 == 0

            mine_in, other_in = descend(z, where, candidates, lefts[level], cross)
            candidates, cross = [mine_in, send(other_in, others(level, 0))], None
        candidates.append(send(other_in, others(2, 1)))
        near = tree.pairs(lambda odd: [(tree.root(odd, 2, g), tree.root(odd, 2, g) ^ 1) for g in range(size >> 2)])
        candidates.append(send(mine_in, near))

        def where(seg, tm):
            top, other = top_and_other(seg, tm, 2)
            index = jnp.where(tm == other, 1, jnp.where(tm == other ^ 1, 2, jnp.where(tm == top, 0, 3)))
            return index, tm % 2 == 1

        return last_steps(z, where, candidates, left, transition, drive), ends

    return per_device


def solution(mesh):
    return jax.shard_map(
        make(mesh),
        mesh=mesh,
        in_specs=(
            P(("seg", "tm"), None, None),
            P(("seg", "tm"), None, None),
            P(("seg", "tm"), None, None),
            P(),
            P("tm", None),
        ),
        out_specs=(P(("seg", "tm"), None, None), P("seg", "tm", None)),
        check_vma=False,
    )
```

```python
import jax
import jax.numpy as jnp
from jax import lax
from jax.experimental import pallas as pl
from jax.experimental.pallas import tpu as pltpu
from jax.sharding import PartitionSpec as P

F32 = jnp.float32
BF16 = jnp.bfloat16
AXES = ("seg", "tm")
GRANT = 10 * 1024 * 1024
AHEAD = 2


def halves(x):
    hi = x.astype(BF16)
    return hi, (x - hi.astype(F32)).astype(BF16)


def dot(a, b):
    return jnp.dot(a, b, preferred_element_type=F32)


def dot3(a_hi, a_lo, b_hi, b_lo):
    return dot(a_hi, b_hi) + (dot(a_hi, b_lo) + dot(a_lo, b_hi))


def few(rows, hi, lo=None):
    r_hi = rows.astype(BF16)
    r_hi32 = r_hi.astype(F32)
    both = jnp.concatenate([r_hi32, rows - r_hi32]).astype(BF16)
    res = dot(both, hi)
    res = res[: rows.shape[0]] + res[rows.shape[0] :]
    return res if lo is None else res + dot(r_hi, lo)


class Sizes:
    def __init__(self, width, series, chunks):
        self.width, self.series, self.chunks = width, series, chunks
        self.part = width // chunks
        self.tall = width + 16 * (-(-series // 16))
        self.buf = width + 8 * (-(-chunks * series // 8))
        self.low = self.tall - width


def put_rows(z, out, body, tail):
    for j in range(z.chunks):
        cols = slice(j * z.part, (j + 1) * z.part)
        out[j * z.part : (j + 1) * z.part, :] = body[:, cols]
        out[z.width + j * z.series : z.width + (j + 1) * z.series, :] = tail[:, cols]


def put_cols(z, out, body, tail):
    out[: z.width, :] = body
    out[z.width : z.width + z.series, :] = tail


def gather_rows(z, bufs, full):
    for k, buf in enumerate(bufs):
        for j in range(z.chunks):
            full[k * z.part : (k + 1) * z.part, j * z.part : (j + 1) * z.part] = buf[j * z.part : (j + 1) * z.part, :]
    for j in range(z.chunks):
        full[z.width : z.width + z.series, j * z.part : (j + 1) * z.part] = bufs[0][
            z.width + j * z.series : z.width + (j + 1) * z.series, :
        ]


def gather_cols(z, bufs, full):
    for k, buf in enumerate(bufs):
        cols = slice(k * z.part, (k + 1) * z.part)
        full[: z.width, cols] = buf[: z.width, :]
        full[z.width : z.width + z.series, cols] = buf[z.width : z.width + z.series, :]


def clear_low(z, full):
    full[z.width :, :] = jnp.zeros((z.low, z.width), F32)


def put_chunks(z, by_rows, outs, full):
    @pl.when(by_rows)
    def _():
        for k, out in enumerate(outs):
            put_rows(z, out, full[k * z.part : (k + 1) * z.part, :], full[z.width : z.width + z.series, :])

    @pl.when(jnp.logical_not(by_rows))
    def _():
        for k, out in enumerate(outs):
            cols = slice(k * z.part, (k + 1) * z.part)
            put_cols(z, out, full[: z.width, cols], full[z.width : z.width + z.series, cols])


def call(kernel, outs, operands, where=None, scratch=(), far=0):
    in_specs = [pl.BlockSpec(memory_space=pltpu.HBM if i < far else pltpu.VMEM) for i in range(len(operands))]
    operands = [pltpu.with_memory_space_constraint(x, pltpu.HBM) if i < far else x for i, x in enumerate(operands)]

    def body(*refs):
        if where is None:
            kernel(*refs)
        else:
            kernel(where(lax.axis_index("seg"), lax.axis_index("tm")), *refs)

    return pl.pallas_call(
        body,
        out_shape=outs,
        in_specs=in_specs,
        out_specs=jax.tree.map(lambda _: pl.BlockSpec(memory_space=pltpu.VMEM), outs),
        scratch_shapes=list(scratch),
        compiler_params=pltpu.CompilerParams(vmem_limit_bytes=GRANT),
    )(*operands)


def shape(rows, cols, dtype=F32):
    return jax.ShapeDtypeStruct((rows, cols), dtype)


def gather(z, by_rows, bufs, full):
    @pl.when(by_rows)
    def _():
        gather_rows(z, bufs, full)

    @pl.when(jnp.logical_not(by_rows))
    def _():
        gather_cols(z, bufs, full)


def map_shapes(z):
    return [shape(z.tall, z.width, BF16), shape(z.tall, z.width, BF16), shape(z.series, z.width)]


def local_map(z, where, transition, gain, observed):
    steps = transition.shape[0]

    def kernel(by_rows, t_hbm, g_hbm, o_hbm, *rest):
        chunks, (whole, hi, lo, tail, drive) = rest[: z.chunks], rest[z.chunks : z.chunks + 5]
        t, g, o, sems = rest[z.chunks + 5 :]
        copies = [
            pltpu.make_async_copy(t_hbm, t, sems.at[0]),
            pltpu.make_async_copy(g_hbm, g, sems.at[1]),
            pltpu.make_async_copy(o_hbm, o, sems.at[2]),
        ]
        for copy in copies:
            copy.start()
        copies[0].wait()
        body = t[0]
        for i in range(1, steps):
            if i == 1:
                body = dot(body, t[i])
            else:
                b_hi, b_lo = halves(body)
                body = dot(b_hi, t[i]) + dot(b_lo, t[i])
        clear_low(z, whole)
        whole[: z.width, :] = body.astype(F32)
        copies[1].wait()
        copies[2].wait()
        drives = [dot(o[i], g[i]) for i in range(steps)]
        low = drives[0]
        for i in range(steps):
            drive[i] = drives[i]
            if i:
                l_hi, l_lo = halves(low)
                low = dot(l_hi, t[i]) + dot(l_lo, t[i]) + drives[i]
        whole[z.width : z.width + z.series, :] = low
        tail[...] = low
        put_chunks(z, by_rows, chunks, whole)
        hi[...], lo[...] = halves(whole[...])

    res = call(
        kernel,
        [shape(z.buf, z.part)] * z.chunks
        + [shape(z.tall, z.width)]
        + map_shapes(z)
        + [jax.ShapeDtypeStruct((steps, z.series, z.width), F32)],
        [transition, gain, observed],
        where,
        scratch=[
            pltpu.VMEM(transition.shape, transition.dtype),
            pltpu.VMEM(gain.shape, gain.dtype),
            pltpu.VMEM(observed.shape, observed.dtype),
            pltpu.SemaphoreType.DMA((3,)),
        ],
        far=3,
    )
    n = z.chunks
    return res[:n], res[n], tuple(res[n + 1 : n + 4]), res[n + 4]


def times_chunk(z, where, chunk, own):
    def kernel(by_rows, got, own_hi, own_lo, own_tail, out, left):
        @pl.when(by_rows)
        def _():
            left[z.part :, :] = jnp.zeros((left.shape[0] - z.part, z.width), F32)
            for j in range(z.chunks):
                cols = slice(j * z.part, (j + 1) * z.part)
                left[: z.part, cols] = got[j * z.part : (j + 1) * z.part, :]
                left[z.part : z.part + z.series, cols] = got[z.width + j * z.series : z.width + (j + 1) * z.series, :]
            l_hi, l_lo = halves(left[...])
            res = dot3(l_hi, l_lo, own_hi[: z.width, :], own_lo[: z.width, :])
            put_rows(z, out, res[: z.part], res[z.part : z.part + z.series] + own_tail[...])

        @pl.when(jnp.logical_not(by_rows))
        def _():
            r_hi, r_lo = halves(got[: z.width, :])
            res = dot3(own_hi[...], own_lo[...], r_hi, r_lo)
            out[z.width :, :] = jnp.zeros((z.buf - z.width, z.part), F32)
            put_cols(z, out, res[: z.width], res[z.width : z.width + z.series] + got[z.width : z.width + z.series, :])

    return call(
        kernel, shape(z.buf, z.part), [chunk, *own], where, scratch=[pltpu.VMEM((z.part + z.low, z.width), F32)]
    )


def merge(z, where, got, own):
    def kernel(flag, *refs):
        by_rows, got_left, next_rows = flag
        n = z.chunks
        gots, owns = refs[:n], refs[n : 2 * n]
        outs = refs[2 * n : 3 * n]
        hi, lo, tail, left_hi, left_lo, left_tail = refs[3 * n : 3 * n + 6]
        a, b, c = refs[3 * n + 6 :]
        clear_low(z, a)
        clear_low(z, b)

        @pl.when(got_left)
        def _():
            gather(z, by_rows, gots, a)
            gather(z, by_rows, owns, b)

        @pl.when(jnp.logical_not(got_left))
        def _():
            gather(z, by_rows, owns, a)
            gather(z, by_rows, gots, b)

        left_hi[...], left_lo[...] = halves(a[...])
        left_tail[...] = a[z.width : z.width + z.series, :]
        r_hi, r_lo = halves(b[: z.width, :])
        c[...] = dot3(left_hi[...], left_lo[...], r_hi, r_lo)
        c[z.width : z.width + z.series, :] = c[z.width : z.width + z.series, :] + b[z.width : z.width + z.series, :]
        put_chunks(z, next_rows, outs, c)
        hi[...], lo[...] = halves(c[...])
        tail[...] = c[z.width : z.width + z.series, :]

    res = call(
        kernel,
        [shape(z.buf, z.part)] * z.chunks + map_shapes(z) * 2,
        list(got) + list(own),
        where,
        scratch=[pltpu.VMEM((z.tall, z.width), F32)] * 3,
    )
    n = z.chunks
    return res[:n], tuple(res[n : n + 3]), tuple(res[n + 3 :])


def assemble(z, where, chunks, others=None):
    extra = [] if others is None else list(others)

    def kernel(flag, *refs):
        by_rows, swap = flag
        n = z.chunks
        bufs, rest = refs[:n], refs[n : n + len(extra)]
        hi, lo, tail, full = refs[n + len(extra) :]
        clear_low(z, full)
        if not extra:
            gather(z, by_rows, bufs, full)
        else:

            @pl.when(jnp.logical_not(swap))
            def _():
                gather(z, by_rows, bufs, full)

            @pl.when(swap)
            def _():
                if len(rest) == 1:
                    full[...] = rest[0][...]
                else:
                    gather(z, by_rows, rest, full)

        hi[...], lo[...] = halves(full[...])
        tail[...] = full[z.width : z.width + z.series, :]

    return call(kernel, map_shapes(z), list(chunks) + extra, where, scratch=[pltpu.VMEM((z.tall, z.width), F32)])


def padded(series):
    return 8 * (-(-series // 8))


def advance(z, where, parts, block, before=None, split=False):
    low = padded(z.series)
    joined = len(parts) == 1
    rows = parts[0].shape[0] - low if joined else sum(p.shape[0] for p in parts[:-1])
    operands = list(parts) + list(block) + ([] if before is None else [before])

    def kernel(active, *refs):
        given, (hi, lo, tail) = refs[: len(parts)], refs[len(parts) : len(parts) + 3]
        outs, now = refs[len(operands) : -1], refs[-1]

        def put(value):
            if split:
                outs[0][...] = value[: rows // 2]
                outs[1][...] = value[rows // 2 : rows]
            else:
                outs[0][...] = value

        def run():
            if joined:
                state = given[0][...]
            else:
                now[rows:, :] = jnp.zeros((low, z.width), F32)
                at = 0
                for part in given:
                    now[at : at + part.shape[0], :] = part[...]
                    at += part.shape[0]
                state = now[...]
            now[...] = few(state, hi[: z.width, :], lo[: z.width, :])
            now[rows : rows + z.series, :] = now[rows : rows + z.series, :] + tail[...]
            put(now[...])

        if before is None:
            run()
        else:
            pl.when(active)(run)

            @pl.when(jnp.logical_not(active))
            def _():
                put(refs[len(operands) - 1][...])

    outs = [shape(rows // 2, z.width)] * 2 if split else [shape(rows + low, z.width)]
    res = call(kernel, outs, operands, where, scratch=[pltpu.VMEM((rows + low, z.width), F32)])
    return res if split else res[0]


def deal(where, kept, got):
    def kernel(received, a, b, out):
        @pl.when(received)
        def _():
            out[0] = b[...]

        @pl.when(jnp.logical_not(received))
        def _():
            out[0] = a[...]

    return call(kernel, jax.ShapeDtypeStruct((1, *kept.shape), F32), [kept, got], where)


def load_choice(z, index, refs, into):
    for i, ref in enumerate(refs):

        @pl.when(index == i)
        def _():
            if ref.shape[0] == z.series:
                into[...] = jnp.zeros(into.shape, F32)
                into[: z.series, :] = ref[...]
            else:
                into[...] = ref[ref.shape[0] - into.shape[0] :, :]


def descend(z, where, candidates, left, cross=None):
    low = padded(z.series)
    m = len(candidates)
    maps = list(left) + ([] if cross is None else list(cross))

    def kernel(flag, *refs):
        index, through, in_right = flag
        hi, lo, tail = refs[m : m + 3]
        mine, other, now = refs[m + len(maps) :]
        load_choice(z, index, refs[:m], now)
        if cross is not None:

            @pl.when(through)
            def _():
                c_hi, c_lo, c_tail = refs[m + 3 : m + 6]
                now[...] = few(now[...], c_hi[: z.width, :], c_lo[: z.width, :])
                now[: z.series, :] = now[: z.series, :] + c_tail[...]

        beyond = few(now[...], hi[: z.width, :], lo[: z.width, :])

        @pl.when(in_right)
        def _():
            mine[...] = beyond
            mine[: z.series, :] = mine[: z.series, :] + tail[...]
            other[...] = now[...]

        @pl.when(jnp.logical_not(in_right))
        def _():
            other[...] = beyond
            other[: z.series, :] = other[: z.series, :] + tail[...]
            mine[...] = now[...]

    return call(
        kernel, [shape(low, z.width)] * 2, [*candidates, *maps], where, scratch=[pltpu.VMEM((low, z.width), F32)]
    )


def last_steps(z, where, candidates, left, transition, drive):
    steps = transition.shape[0]
    m = len(candidates)
    low = padded(z.series)

    def kernel(flag, *refs):
        index, through = flag
        hi, lo, tail, t, d, out, now = refs[m:]
        load_choice(z, index, refs[:m], now)

        @pl.when(through)
        def _():
            now[...] = few(now[...], hi[: z.width, :], lo[: z.width, :])
            now[: z.series, :] = now[: z.series, :] + tail[...]

        for i in range(steps):
            now[...] = few(now[...], t[i])
            now[: z.series, :] = now[: z.series, :] + d[i]
            out[i] = now[: z.series, :]

    return call(
        kernel,
        jax.ShapeDtypeStruct((steps, z.series, z.width), F32),
        [*candidates, *left, transition, drive],
        where,
        scratch=[pltpu.VMEM((low, z.width), F32)],
    )


class Tree:
    def __init__(self, segs, size):
        self.segs, self.size = segs, size
        self.depth = size.bit_length() - 1
        if size != 1 << self.depth or self.depth < 3:
            raise ValueError("tm size")

    def root(self, odd, level, group):
        if level == 1:
            return 2 * group + (0 if odd else 1)
        return self.root(odd, level - 1, 2 * group + (1 - group % 2))

    def pairs(self, per_parity):
        return [
            (s * self.size + a, s * self.size + b) for s in range(self.segs) for a, b in per_parity(s % 2)
        ]

    def child_roots(self, odd, level, group):
        return self.root(odd, level - 1, 2 * group), self.root(odd, level - 1, 2 * group + 1)

    def up(self, level):
        def of(odd):
            if level == 1:
                return [(i, i ^ 1) for i in range(self.size) if i % 2 == (1 if odd else 0)]
            found = []
            for g in range(self.size >> level):
                a, b = self.child_roots(odd, level, g)
                if level == self.depth:
                    found += [(a, b), (b, a)]
                else:
                    found.append((a, b) if g % 2 == 0 else (b, a))
            return found

        return self.pairs(of)

    def far(self, bit, seg=None):
        found = []
        for s in range(self.segs) if seg is None else [seg]:
            for i in range(self.size):
                away = i // 2 ^ self.root(0, self.depth - 1, 2 * i // self.size) // 2
                if bit <= away < 2 * bit:
                    found.append((s * self.size + i, s * self.size + (i ^ 2 * bit)))
        return found

    def holds(self, i):
        return i // 2 == self.root(0, self.depth - 1, 2 * i // self.size) // 2

    def root_of(self, odd, level, group):
        for _ in range(level - 1):
            group = 2 * group + 1 - group % 2
        return 2 * group + 1 - odd


def tied(x, after):
    return lax.optimization_barrier((x, after))[0]


def make(mesh):
    segs, size = mesh.shape["seg"], mesh.shape["tm"]
    tree = Tree(segs, size)
    depth = tree.depth
    half = size // 2

    def send(x, pairs):
        return lax.ppermute(x, AXES, pairs)

    def others(level, flip):
        def of(odd):
            found = []
            for g in range(size >> level):
                root = tree.root(odd, level, g)
                a, b = tree.child_roots(odd, level, g)
                found.append((root, (a if root == b else b) ^ flip))
            return found

        return tree.pairs(of)

    def top_and_other(seg, tm, level):
        odd, group = seg % 2, tm >> level
        top = tree.root_of(odd, level, group)
        a, b = (tree.root_of(odd, level - 1, 2 * group + i) for i in (0, 1))
        return top, a + b - top

    def per_device(transition, obs_gain, observed, init_mean, init_factor):
        width, series = transition.shape[1], observed.shape[1]
        chunks = next(n for n in (4, 2, 1) if width % (n * 128) == 0 or n == 1)
        z = Sizes(width, series, chunks)

        def is_even(seg, tm):
            return seg % 2 == 0

        def in_right_half(seg, tm):
            return tm >= half

        own, whole, own_map, drive = local_map(z, is_even, transition, obs_gain, observed)
        first = [send(c, tree.up(1)) for c in own]
        outs = [times_chunk(z, is_even, c, own_map) for c in first]
        back = send(tied(whole, outs), tree.pairs(lambda odd: [(i, i + 1) for i in range(0, size, 2)] if odd else []))
        bits = [1 << i for i in range(depth - 3, -1, -1)]
        start = [init_factor]
        for bit in bits:
            held = start[0] if len(start) == 1 else jnp.concatenate(start)
            start = [held, send(tied(held, outs), tree.far(bit, 0))]
        lefts = {}
        for level in range(2, depth):

            def where(seg, tm, level=level):
                by_rows = seg % 2 == 0 if level == 2 else seg >= 0
                next_rows = tm < half if level == depth - 1 else seg >= 0
                return by_rows, (tm >> level) % 2 == 0, next_rows

            got = [send(c, tree.up(level)) for c in outs]
            outs, mine, lefts[level] = merge(z, where, got, outs)
        crossed, final = [], []
        for k, c in enumerate(outs):
            sent = c if k < AHEAD else tied(c, final[k - AHEAD])
            crossed.append(send(sent, tree.up(depth)))
            final.append(times_chunk(z, in_right_half, crossed[k], mine))
        roots = tree.pairs(lambda odd: [(r, r ^ 1) for r in tree.child_roots(odd, depth, 0)])
        got = [send(c, roots) for c in final]
        left = assemble(z, lambda seg, tm: (seg >= 0, seg % 2 == 1), first, [back])
        halfway = assemble(z, lambda seg, tm: (seg >= 0, seg < 0), crossed)
        got[-1], left, halfway = lax.optimization_barrier((got[-1], left, halfway))

        def beside(seg, tm):
            return tm >= half, tm ^ 1 == tree.root_of(seg % 2, depth - 1, tm // half)

        block = assemble(z, beside, final, got)

        arrived, moved = [], [advance(z, lambda seg, tm: seg >= 0, [*start, init_mean], block)]
        for turn in range(1, segs):
            pairs = [((turn - 1) * size + i, turn * size + i) for i in range(size) if tree.holds(i)]
            arrived.append(send(moved[-1], pairs))

            def where(seg, tm, turn=turn):
                return seg >= turn

            moved.append(advance(z, where, [arrived[-1]], block, moved[-1], turn == segs - 1))

        candidates, cross = [init_mean, *arrived], halfway
        for level in range(depth - 1, 1, -1):

            def where(seg, tm, level=level):
                if level == depth - 1:
                    index = seg
                else:
                    index = (tm == top_and_other(seg, tm, level + 1)[1]).astype(jnp.int32)
                return index, tm >= half, (tm >> level) % 2 == 0

            mine_in, other_in = descend(z, where, candidates, lefts[level], cross)
            candidates, cross = [mine_in, send(other_in, others(level, 0))], None
        candidates.append(send(other_in, others(2, 1)))
        near = tree.pairs(lambda odd: [(tree.root(odd, 2, g), tree.root(odd, 2, g) ^ 1) for g in range(size >> 2)])
        candidates.append(send(mine_in, near))

        kept, given = moved[-1]
        for bit in reversed(bits):
            back_pairs = [(b, a) for a, b in tree.far(bit)]
            came = send(given, back_pairs)

            def where(seg, tm, bit=bit):
                away = tm // 2 ^ tree.root_of(0, depth - 1, tm // half) // 2
                return (away >= bit) & (away < 2 * bit)

            kept = deal(where, kept, came)
            if bit != bits[0]:
                rows = kept.shape[1] // 2
                kept, given = kept[0, :rows], kept[0, rows:]
        ends = kept

        def where(seg, tm):
            top, other = top_and_other(seg, tm, 2)
            index = jnp.where(tm == other, 1, jnp.where(tm == other ^ 1, 2, jnp.where(tm == top, 0, 3)))
            return index, tm % 2 == 1

        return last_steps(z, where, candidates, left, transition, drive), ends

    return per_device


def solution(mesh):
    return jax.shard_map(
        make(mesh),
        mesh=mesh,
        in_specs=(
            P(("seg", "tm"), None, None),
            P(("seg", "tm"), None, None),
            P(("seg", "tm"), None, None),
            P(),
            P("tm", None),
        ),
        out_specs=(P(("seg", "tm"), None, None), P("seg", "tm", None)),
        check_vma=False,
    )
```

```python
import jax
import jax.numpy as jnp
from jax import lax
from jax.experimental import pallas as pl
from jax.experimental.pallas import tpu as pltpu
from jax.sharding import PartitionSpec as P

F32 = jnp.float32
BF16 = jnp.bfloat16
AXES = ("seg", "tm")
GRANT = 10 * 1024 * 1024


def halves(x):
    hi = x.astype(BF16)
    return hi, (x - hi.astype(F32)).astype(BF16)


def dot(a, b):
    return jnp.dot(a, b, preferred_element_type=F32)


def dot3(a_hi, a_lo, b_hi, b_lo):
    return dot(a_hi, b_hi) + (dot(a_hi, b_lo) + dot(a_lo, b_hi))


def few(rows, hi, lo=None):
    r_hi = rows.astype(BF16)
    r_hi32 = r_hi.astype(F32)
    both = jnp.concatenate([r_hi32, rows - r_hi32]).astype(BF16)
    res = dot(both, hi)
    res = res[: rows.shape[0]] + res[rows.shape[0] :]
    return res if lo is None else res + dot(r_hi, lo)


class Sizes:
    def __init__(self, width, series, chunks):
        self.width, self.series, self.chunks = width, series, chunks
        self.part = width // chunks
        self.tall = width + 16 * (-(-series // 16))
        self.buf = width + 8 * (-(-chunks * series // 8))
        self.low = self.tall - width


def put_rows(z, out, body, tail):
    for j in range(z.chunks):
        cols = slice(j * z.part, (j + 1) * z.part)
        out[j * z.part : (j + 1) * z.part, :] = body[:, cols]
        out[z.width + j * z.series : z.width + (j + 1) * z.series, :] = tail[:, cols]


def put_cols(z, out, body, tail):
    out[: z.width, :] = body
    out[z.width : z.width + z.series, :] = tail


def gather_rows(z, bufs, full):
    for k, buf in enumerate(bufs):
        for j in range(z.chunks):
            full[k * z.part : (k + 1) * z.part, j * z.part : (j + 1) * z.part] = buf[j * z.part : (j + 1) * z.part, :]
    for j in range(z.chunks):
        full[z.width : z.width + z.series, j * z.part : (j + 1) * z.part] = bufs[0][
            z.width + j * z.series : z.width + (j + 1) * z.series, :
        ]


def gather_cols(z, bufs, full):
    for k, buf in enumerate(bufs):
        cols = slice(k * z.part, (k + 1) * z.part)
        full[: z.width, cols] = buf[: z.width, :]
        full[z.width : z.width + z.series, cols] = buf[z.width : z.width + z.series, :]


def clear_low(z, full):
    full[z.width :, :] = jnp.zeros((z.low, z.width), F32)


def put_chunks(z, by_rows, outs, full):
    @pl.when(by_rows)
    def _():
        for k, out in enumerate(outs):
            put_rows(z, out, full[k * z.part : (k + 1) * z.part, :], full[z.width : z.width + z.series, :])

    @pl.when(jnp.logical_not(by_rows))
    def _():
        for k, out in enumerate(outs):
            cols = slice(k * z.part, (k + 1) * z.part)
            put_cols(z, out, full[: z.width, cols], full[z.width : z.width + z.series, cols])


def call(kernel, outs, operands, where=None, scratch=(), far=0):
    in_specs = [pl.BlockSpec(memory_space=pltpu.HBM if i < far else pltpu.VMEM) for i in range(len(operands))]
    operands = [pltpu.with_memory_space_constraint(x, pltpu.HBM) if i < far else x for i, x in enumerate(operands)]

    def body(*refs):
        if where is None:
            kernel(*refs)
        else:
            kernel(where(lax.axis_index("seg"), lax.axis_index("tm")), *refs)

    return pl.pallas_call(
        body,
        out_shape=outs,
        in_specs=in_specs,
        out_specs=jax.tree.map(lambda _: pl.BlockSpec(memory_space=pltpu.VMEM), outs),
        scratch_shapes=list(scratch),
        compiler_params=pltpu.CompilerParams(vmem_limit_bytes=GRANT),
    )(*operands)


def shape(rows, cols, dtype=F32):
    return jax.ShapeDtypeStruct((rows, cols), dtype)


def gather(z, by_rows, bufs, full):
    @pl.when(by_rows)
    def _():
        gather_rows(z, bufs, full)

    @pl.when(jnp.logical_not(by_rows))
    def _():
        gather_cols(z, bufs, full)


def map_shapes(z):
    return [shape(z.tall, z.width, BF16), shape(z.tall, z.width, BF16), shape(z.series, z.width)]


def local_map(z, where, transition, gain, observed):
    steps = transition.shape[0]

    def kernel(flag, *refs):
        by_rows, active = flag
        pl.when(active)(lambda: run(by_rows, *refs))

    def run(by_rows, t_hbm, g_hbm, o_hbm, *rest):
        chunks, (whole, hi, lo, tail, drive) = rest[: z.chunks], rest[z.chunks : z.chunks + 5]
        t, g, o, sems = rest[z.chunks + 5 :]
        copies = [
            pltpu.make_async_copy(t_hbm, t, sems.at[0]),
            pltpu.make_async_copy(g_hbm, g, sems.at[1]),
            pltpu.make_async_copy(o_hbm, o, sems.at[2]),
        ]
        for copy in copies:
            copy.start()
        copies[0].wait()
        body = t[0]
        for i in range(1, steps):
            if i == 1:
                body = dot(body, t[i])
            else:
                b_hi, b_lo = halves(body)
                body = dot(b_hi, t[i]) + dot(b_lo, t[i])
        clear_low(z, whole)
        whole[: z.width, :] = body.astype(F32)
        copies[1].wait()
        copies[2].wait()
        drives = [dot(o[i], g[i]) for i in range(steps)]
        low = drives[0]
        for i in range(steps):
            drive[i] = drives[i]
            if i:
                l_hi, l_lo = halves(low)
                low = dot(l_hi, t[i]) + dot(l_lo, t[i]) + drives[i]
        whole[z.width : z.width + z.series, :] = low
        tail[...] = low
        put_chunks(z, by_rows, chunks, whole)
        hi[...], lo[...] = halves(whole[...])

    res = call(
        kernel,
        [shape(z.buf, z.part)] * z.chunks
        + [shape(z.tall, z.width)]
        + map_shapes(z)
        + [jax.ShapeDtypeStruct((steps, z.series, z.width), F32)],
        [transition, gain, observed],
        where,
        scratch=[
            pltpu.VMEM(transition.shape, transition.dtype),
            pltpu.VMEM(gain.shape, gain.dtype),
            pltpu.VMEM(observed.shape, observed.dtype),
            pltpu.SemaphoreType.DMA((3,)),
        ],
        far=3,
    )
    n = z.chunks
    return res[:n], res[n], tuple(res[n + 1 : n + 4]), res[n + 4]


def quarter(z, ref, k):
    return ref.at[pl.ds(k * z.buf, z.buf)]


def split_parts(z, refs):
    return [quarter(z, ref, k) for ref in refs for k in range(ref.shape[0] // z.buf)]


def times_chunk(z, where, chunk, own):
    count = chunk.shape[0] // z.buf
    span = count * z.part

    def kernel(by_rows, got, own_hi, own_lo, own_tail, *rest):
        outs, (left, right) = rest[:count], rest[count:]
        gots = split_parts(z, [got])

        @pl.when(by_rows)
        def _():
            left[span:, :] = jnp.zeros((left.shape[0] - span, z.width), F32)
            for j in range(z.chunks):
                cols = slice(j * z.part, (j + 1) * z.part)
                for q, part in enumerate(gots):
                    left[q * z.part : (q + 1) * z.part, cols] = part[j * z.part : (j + 1) * z.part, :]
                left[span : span + z.series, cols] = gots[0][z.width + j * z.series : z.width + (j + 1) * z.series, :]
            l_hi, l_lo = halves(left[...])
            res = dot3(l_hi, l_lo, own_hi[: z.width, :], own_lo[: z.width, :])
            for q, out in enumerate(outs):
                put_rows(z, out, res[q * z.part : (q + 1) * z.part], res[span : span + z.series] + own_tail[...])

        @pl.when(jnp.logical_not(by_rows))
        def _():
            for q, part in enumerate(gots):
                right[:, q * z.part : (q + 1) * z.part] = part[: z.width + z.series, :]
            r_hi, r_lo = halves(right[: z.width, :])
            res = dot3(own_hi[...], own_lo[...], r_hi, r_lo)
            low = res[z.width : z.width + z.series] + right[z.width : z.width + z.series, :]
            for q, out in enumerate(outs):
                cols = slice(q * z.part, (q + 1) * z.part)
                out[z.width :, :] = jnp.zeros((z.buf - z.width, z.part), F32)
                put_cols(z, out, res[: z.width, cols], low[:, cols])

    return call(
        kernel,
        [shape(z.buf, z.part)] * count,
        [chunk, *own],
        where,
        scratch=[pltpu.VMEM((span + z.low, z.width), F32), pltpu.VMEM((z.width + z.series, span), F32)],
    )


def merge(z, where, got, own, count=None):
    sent = count or z.chunks

    def kernel(flag, *refs):
        by_rows, got_left, next_rows = flag
        n = z.chunks
        gots, owns = refs[:n], refs[n : 2 * n]
        outs = split_parts(z, refs[2 * n : 2 * n + sent])
        hi, lo, tail, left_hi, left_lo, left_tail = refs[2 * n + sent : 2 * n + sent + 6]
        a, b, c = refs[2 * n + sent + 6 :]
        clear_low(z, a)
        clear_low(z, b)

        @pl.when(got_left)
        def _():
            gather(z, by_rows, gots, a)
            gather(z, by_rows, owns, b)

        @pl.when(jnp.logical_not(got_left))
        def _():
            gather(z, by_rows, owns, a)
            gather(z, by_rows, gots, b)

        left_hi[...], left_lo[...] = halves(a[...])
        left_tail[...] = a[z.width : z.width + z.series, :]
        r_hi, r_lo = halves(b[: z.width, :])
        c[...] = dot3(left_hi[...], left_lo[...], r_hi, r_lo)
        c[z.width : z.width + z.series, :] = c[z.width : z.width + z.series, :] + b[z.width : z.width + z.series, :]
        put_chunks(z, next_rows, outs, c)
        hi[...], lo[...] = halves(c[...])
        tail[...] = c[z.width : z.width + z.series, :]

    res = call(
        kernel,
        [shape(z.chunks // sent * z.buf, z.part)] * sent + map_shapes(z) * 2,
        list(got) + list(own),
        where,
        scratch=[pltpu.VMEM((z.tall, z.width), F32)] * 3,
    )
    return res[:sent], tuple(res[sent : sent + 3]), tuple(res[sent + 3 :])


def assemble(z, where, chunks, others=None):
    extra = [] if others is None else list(others)

    def kernel(flag, *refs):
        by_rows, swap = flag
        n = len(chunks)
        bufs, rest = split_parts(z, refs[:n]), refs[n : n + len(extra)]
        hi, lo, tail, full = refs[n + len(extra) :]
        clear_low(z, full)
        if not extra:
            gather(z, by_rows, bufs, full)
        else:

            @pl.when(jnp.logical_not(swap))
            def _():
                gather(z, by_rows, bufs, full)

            @pl.when(swap)
            def _():
                if len(rest) == 1:
                    full[...] = rest[0][...]
                else:
                    gather(z, by_rows, rest, full)

        hi[...], lo[...] = halves(full[...])
        tail[...] = full[z.width : z.width + z.series, :]

    return call(kernel, map_shapes(z), list(chunks) + extra, where, scratch=[pltpu.VMEM((z.tall, z.width), F32)])


def padded(series):
    return 8 * (-(-series // 8))


def advance(z, where, parts, block, before=None, split=False):
    low = padded(z.series)
    joined = len(parts) == 1
    rows = parts[0].shape[0] - low if joined else sum(p.shape[0] for p in parts[:-1])
    operands = list(parts) + list(block) + ([] if before is None else [before])

    def kernel(active, *refs):
        given, (hi, lo, tail) = refs[: len(parts)], refs[len(parts) : len(parts) + 3]
        outs, now = refs[len(operands) : -1], refs[-1]

        def put(value):
            if split:
                outs[0][...] = value[: rows // 2]
                outs[1][...] = value[rows // 2 : rows]
            else:
                outs[0][...] = value

        def run():
            if joined:
                state = given[0][...]
            else:
                now[rows:, :] = jnp.zeros((low, z.width), F32)
                at = 0
                for part in given:
                    now[at : at + part.shape[0], :] = part[...]
                    at += part.shape[0]
                state = now[...]
            now[...] = few(state, hi[: z.width, :], lo[: z.width, :])
            now[rows : rows + z.series, :] = now[rows : rows + z.series, :] + tail[...]
            put(now[...])

        if before is None:
            run()
        else:
            pl.when(active)(run)

            @pl.when(jnp.logical_not(active))
            def _():
                put(refs[len(operands) - 1][...])

    outs = [shape(rows // 2, z.width)] * 2 if split else [shape(rows + low, z.width)]
    res = call(kernel, outs, operands, where, scratch=[pltpu.VMEM((rows + low, z.width), F32)])
    return res if split else res[0]


def deal(where, kept, got):
    def kernel(received, a, b, out):
        @pl.when(received)
        def _():
            out[0] = b[...]

        @pl.when(jnp.logical_not(received))
        def _():
            out[0] = a[...]

    return call(kernel, jax.ShapeDtypeStruct((1, *kept.shape), F32), [kept, got], where)


def load_choice(z, index, refs, into):
    for i, ref in enumerate(refs):

        @pl.when(index == i)
        def _():
            if ref.shape[0] == z.series:
                into[...] = jnp.zeros(into.shape, F32)
                into[: z.series, :] = ref[...]
            else:
                into[...] = ref[ref.shape[0] - into.shape[0] :, :]


def descend(z, where, candidates, left, cross=None):
    low = padded(z.series)
    m = len(candidates)
    maps = list(left) + ([] if cross is None else list(cross))

    def kernel(flag, *refs):
        index, through, in_right = flag
        hi, lo, tail = refs[m : m + 3]
        mine, other, now = refs[m + len(maps) :]
        load_choice(z, index, refs[:m], now)
        if cross is not None:

            @pl.when(through)
            def _():
                c_hi, c_lo, c_tail = refs[m + 3 : m + 6]
                now[...] = few(now[...], c_hi[: z.width, :], c_lo[: z.width, :])
                now[: z.series, :] = now[: z.series, :] + c_tail[...]

        beyond = few(now[...], hi[: z.width, :], lo[: z.width, :])

        @pl.when(in_right)
        def _():
            mine[...] = beyond
            mine[: z.series, :] = mine[: z.series, :] + tail[...]
            other[...] = now[...]

        @pl.when(jnp.logical_not(in_right))
        def _():
            other[...] = beyond
            other[: z.series, :] = other[: z.series, :] + tail[...]
            mine[...] = now[...]

    return call(
        kernel, [shape(low, z.width)] * 2, [*candidates, *maps], where, scratch=[pltpu.VMEM((low, z.width), F32)]
    )


def last_steps(z, where, candidates, left, transition, drives):
    steps = transition.shape[0]
    m = len(candidates)
    low = padded(z.series)

    def kernel(flag, *refs):
        index, through, second = flag
        hi, lo, tail, t, d0, d1, out, now = refs[m:]
        load_choice(z, index, refs[:m], now)

        @pl.when(through)
        def _():
            now[...] = few(now[...], hi[: z.width, :], lo[: z.width, :])
            now[: z.series, :] = now[: z.series, :] + tail[...]

        for i in range(steps):
            now[...] = few(now[...], t[i])
            now[: z.series, :] = now[: z.series, :] + jnp.where(second, d1[i], d0[i])
            out[i] = now[: z.series, :]

    return call(
        kernel,
        jax.ShapeDtypeStruct((steps, z.series, z.width), F32),
        [*candidates, *left, transition, *drives],
        where,
        scratch=[pltpu.VMEM((low, z.width), F32)],
    )


class Tree:
    def __init__(self, segs, size):
        self.segs, self.size = segs, size
        self.depth = size.bit_length() - 1
        if size != 1 << self.depth or self.depth < 3:
            raise ValueError("tm size")

    def root(self, odd, level, group):
        if level == 1:
            return 2 * group + (0 if odd else 1)
        return self.root(odd, level - 1, 2 * group + (1 - group % 2))

    def pairs(self, per_parity):
        return [
            (s * self.size + a, s * self.size + b) for s in range(self.segs) for a, b in per_parity(s % 2)
        ]

    def child_roots(self, odd, level, group):
        return self.root(odd, level - 1, 2 * group), self.root(odd, level - 1, 2 * group + 1)

    def up(self, level):
        def of(odd):
            if level == 1:
                return [(i, i ^ 1) for i in range(self.size) if i % 2 == (1 if odd else 0)]
            found = []
            for g in range(self.size >> level):
                a, b = self.child_roots(odd, level, g)
                if level == self.depth:
                    found += [(a, b), (b, a)]
                else:
                    found.append((a, b) if g % 2 == 0 else (b, a))
            return found

        return self.pairs(of)

    def far(self, bit, seg=None):
        found = []
        for s in range(self.segs) if seg is None else [seg]:
            for i in range(self.size):
                away = i // 2 ^ self.root(0, self.depth - 1, 2 * i // self.size) // 2
                if bit <= away < 2 * bit:
                    found.append((s * self.size + i, s * self.size + (i ^ 2 * bit)))
        return found

    def holds(self, i):
        return i // 2 == self.root(0, self.depth - 1, 2 * i // self.size) // 2

    def root_of(self, odd, level, group):
        for _ in range(level - 1):
            group = 2 * group + 1 - group % 2
        return 2 * group + 1 - odd


def tied(x, after):
    return lax.optimization_barrier((x, after))[0]


def make(mesh):
    segs, size = mesh.shape["seg"], mesh.shape["tm"]
    tree = Tree(segs, size)
    depth = tree.depth
    half = size // 2

    def send(x, pairs):
        return lax.ppermute(x, AXES, pairs)

    def others(level, flip):
        def of(odd):
            found = []
            for g in range(size >> level):
                root = tree.root(odd, level, g)
                a, b = tree.child_roots(odd, level, g)
                found.append((root, (a if root == b else b) ^ flip))
            return found

        return tree.pairs(of)

    def top_and_other(seg, tm, level):
        odd, group = seg % 2, tm >> level
        top = tree.root_of(odd, level, group)
        a, b = (tree.root_of(odd, level - 1, 2 * group + i) for i in (0, 1))
        return top, a + b - top

    def per_device(transition, obs_gain, observed, init_mean, init_factor):
        width, series = transition.shape[1], observed.shape[1]
        chunks = next(n for n in (4, 2, 1) if width % (n * 128) == 0 or n == 1)
        z = Sizes(width, series, chunks)

        def is_even(seg, tm):
            return seg % 2 == 0

        def in_right_half(seg, tm):
            return tm >= half

        def sends(seg, tm):
            return seg % 2 == 0, (seg + tm) % 2 == 0

        def receives(seg, tm):
            return seg % 2 == 0, (seg + tm) % 2 == 1

        def one_chunk(c):
            return times_chunk(z, is_even, c, own_map)[0]

        own, _, _, early = local_map(z, sends, transition, obs_gain, observed)
        first = [send(c, tree.up(1)) for c in own]
        _, whole, own_map, late = local_map(z, receives, transition, obs_gain, observed)
        outs = [one_chunk(c) for c in first]
        back = send(tied(whole, outs), tree.pairs(lambda odd: [(i, i + 1) for i in range(0, size, 2)] if odd else []))
        bits = [1 << i for i in range(depth - 3, -1, -1)]
        start = [init_factor]
        for bit in bits:
            held = start[0] if len(start) == 1 else jnp.concatenate(start)
            start = [held, send(tied(held, outs), tree.far(bit, 0))]
        lefts = {}
        for level in range(2, depth):

            def where(seg, tm, level=level):
                by_rows = seg % 2 == 0 if level == 2 else seg >= 0
                next_rows = tm < half if level == depth - 1 else seg >= 0
                return by_rows, (tm >> level) % 2 == 0, next_rows

            got = [send(c, tree.up(level)) for c in outs]
            count = min(2, chunks) if level == depth - 1 else None
            outs, mine, lefts[level] = merge(z, where, got, outs, count)
        crossed = [send(c, tree.up(depth)) for c in outs]
        final = [part for c in crossed for part in times_chunk(z, in_right_half, c, mine)]
        roots = tree.pairs(lambda odd: [(r, r ^ 1) for r in tree.child_roots(odd, depth, 0)])
        got = [send(c, roots) for c in final]
        left = assemble(z, lambda seg, tm: (seg >= 0, seg % 2 == 1), first, [back])
        halfway = assemble(z, lambda seg, tm: (seg >= 0, seg < 0), crossed)
        got[-1], left, halfway = lax.optimization_barrier((got[-1], left, halfway))

        def beside(seg, tm):
            return tm >= half, tm ^ 1 == tree.root_of(seg % 2, depth - 1, tm // half)

        block = assemble(z, beside, final, got)

        arrived, moved = [], [advance(z, lambda seg, tm: seg >= 0, [*start, init_mean], block)]
        for turn in range(1, segs):
            pairs = [((turn - 1) * size + i, turn * size + i) for i in range(size) if tree.holds(i)]
            arrived.append(send(moved[-1], pairs))

            def where(seg, tm, turn=turn):
                return seg >= turn

            moved.append(advance(z, where, [arrived[-1]], block, moved[-1], turn == segs - 1))

        candidates, cross = [init_mean, *arrived], halfway
        for level in range(depth - 1, 1, -1):

            def where(seg, tm, level=level):
                if level == depth - 1:
                    index = seg
                else:
                    index = (tm == top_and_other(seg, tm, level + 1)[1]).astype(jnp.int32)
                return index, tm >= half, (tm >> level) % 2 == 0

            mine_in, other_in = descend(z, where, candidates, lefts[level], cross)
            candidates, cross = [mine_in, send(other_in, others(level, 0))], None
        candidates.append(send(other_in, others(2, 1)))
        near = tree.pairs(lambda odd: [(tree.root(odd, 2, g), tree.root(odd, 2, g) ^ 1) for g in range(size >> 2)])
        candidates.append(send(mine_in, near))

        kept, given = moved[-1]
        for bit in reversed(bits):
            back_pairs = [(b, a) for a, b in tree.far(bit)]
            came = send(given, back_pairs)

            def where(seg, tm, bit=bit):
                away = tm // 2 ^ tree.root_of(0, depth - 1, tm // half) // 2
                return (away >= bit) & (away < 2 * bit)

            kept = deal(where, kept, came)
            if bit != bits[0]:
                rows = kept.shape[1] // 2
                kept, given = kept[0, :rows], kept[0, rows:]
        ends = kept

        def where(seg, tm):
            top, other = top_and_other(seg, tm, 2)
            index = jnp.where(tm == other, 1, jnp.where(tm == other ^ 1, 2, jnp.where(tm == top, 0, 3)))
            return index, tm % 2 == 1, (seg + tm) % 2 == 1

        return last_steps(z, where, candidates, left, transition, (early, late)), ends

    return per_device


def solution(mesh):
    return jax.shard_map(
        make(mesh),
        mesh=mesh,
        in_specs=(
            P(("seg", "tm"), None, None),
            P(("seg", "tm"), None, None),
            P(("seg", "tm"), None, None),
            P(),
            P("tm", None),
        ),
        out_specs=(P(("seg", "tm"), None, None), P("seg", "tm", None)),
        check_vma=False,
    )
```

```python
import jax
import jax.numpy as jnp
from jax import lax
from jax.experimental import pallas as pl
from jax.experimental.pallas import tpu as pltpu
from jax.sharding import PartitionSpec as P

F32 = jnp.float32
BF16 = jnp.bfloat16
AXES = ("seg", "tm")
GRANT = 10 * 1024 * 1024


def halves(x):
    hi = x.astype(BF16)
    return hi, (x - hi.astype(F32)).astype(BF16)


def dot(a, b):
    return jnp.dot(a, b, preferred_element_type=F32)


def dot3(a_hi, a_lo, b_hi, b_lo):
    return dot(a_hi, b_hi) + (dot(a_hi, b_lo) + dot(a_lo, b_hi))


def few(rows, hi, lo=None):
    r_hi = rows.astype(BF16)
    r_hi32 = r_hi.astype(F32)
    both = jnp.concatenate([r_hi32, rows - r_hi32]).astype(BF16)
    res = dot(both, hi)
    res = res[: rows.shape[0]] + res[rows.shape[0] :]
    return res if lo is None else res + dot(r_hi, lo)


class Sizes:
    def __init__(self, width, series, chunks):
        self.width, self.series, self.chunks = width, series, chunks
        self.part = width // chunks
        self.tall = width + 16 * (-(-series // 16))
        self.buf = width + 8 * (-(-chunks * series // 8))
        self.low = self.tall - width


def put_rows(z, out, body, tail):
    for j in range(z.chunks):
        cols = slice(j * z.part, (j + 1) * z.part)
        out[j * z.part : (j + 1) * z.part, :] = body[:, cols]
        out[z.width + j * z.series : z.width + (j + 1) * z.series, :] = tail[:, cols]


def put_cols(z, out, body, tail):
    out[: z.width, :] = body
    out[z.width : z.width + z.series, :] = tail


def gather_rows(z, bufs, full):
    for k, buf in enumerate(bufs):
        for j in range(z.chunks):
            full[k * z.part : (k + 1) * z.part, j * z.part : (j + 1) * z.part] = buf[j * z.part : (j + 1) * z.part, :]
    for j in range(z.chunks):
        full[z.width : z.width + z.series, j * z.part : (j + 1) * z.part] = bufs[0][
            z.width + j * z.series : z.width + (j + 1) * z.series, :
        ]


def gather_cols(z, bufs, full):
    for k, buf in enumerate(bufs):
        cols = slice(k * z.part, (k + 1) * z.part)
        full[: z.width, cols] = buf[: z.width, :]
        full[z.width : z.width + z.series, cols] = buf[z.width : z.width + z.series, :]


def clear_low(z, full):
    full[z.width :, :] = jnp.zeros((z.low, z.width), F32)


def put_chunks(z, by_rows, outs, full):
    @pl.when(by_rows)
    def _():
        for k, out in enumerate(outs):
            put_rows(z, out, full[k * z.part : (k + 1) * z.part, :], full[z.width : z.width + z.series, :])

    @pl.when(jnp.logical_not(by_rows))
    def _():
        for k, out in enumerate(outs):
            cols = slice(k * z.part, (k + 1) * z.part)
            put_cols(z, out, full[: z.width, cols], full[z.width : z.width + z.series, cols])


def call(kernel, outs, operands, where=None, scratch=(), far=0):
    in_specs = [pl.BlockSpec(memory_space=pltpu.HBM if i < far else pltpu.VMEM) for i in range(len(operands))]
    operands = [pltpu.with_memory_space_constraint(x, pltpu.HBM) if i < far else x for i, x in enumerate(operands)]

    def body(*refs):
        if where is None:
            kernel(*refs)
        else:
            kernel(where(lax.axis_index("seg"), lax.axis_index("tm")), *refs)

    return pl.pallas_call(
        body,
        out_shape=outs,
        in_specs=in_specs,
        out_specs=jax.tree.map(lambda _: pl.BlockSpec(memory_space=pltpu.VMEM), outs),
        scratch_shapes=list(scratch),
        compiler_params=pltpu.CompilerParams(vmem_limit_bytes=GRANT),
    )(*operands)


def shape(rows, cols, dtype=F32):
    return jax.ShapeDtypeStruct((rows, cols), dtype)


def gather(z, by_rows, bufs, full):
    @pl.when(by_rows)
    def _():
        gather_rows(z, bufs, full)

    @pl.when(jnp.logical_not(by_rows))
    def _():
        gather_cols(z, bufs, full)


def map_shapes(z):
    return [shape(z.tall, z.width, BF16), shape(z.tall, z.width, BF16), shape(z.series, z.width)]


def local_map(z, where, transition, gain, observed, sender):
    steps = transition.shape[0]
    count = z.chunks if sender else 4

    def kernel(flag, *refs):
        by_rows, active = flag
        pl.when(active)(lambda: run(by_rows, *refs))

    def run(by_rows, t_hbm, g_hbm, o_hbm, *rest):
        outs, drive, t, g, o, sems = rest[:count], *rest[count : count + 5]
        whole = rest[-1] if sender else outs[0]
        copies = [
            pltpu.make_async_copy(t_hbm, t, sems.at[0]),
            pltpu.make_async_copy(g_hbm, g, sems.at[1]),
            pltpu.make_async_copy(o_hbm, o, sems.at[2]),
        ]
        for copy in copies:
            copy.start()
        copies[0].wait()
        body = t[0]
        for i in range(1, steps):
            if i == 1:
                body = dot(body, t[i])
            else:
                b_hi, b_lo = halves(body)
                body = dot(b_hi, t[i]) + dot(b_lo, t[i])
        clear_low(z, whole)
        whole[: z.width, :] = body.astype(F32)
        copies[1].wait()
        copies[2].wait()
        drives = [dot(o[i], g[i]) for i in range(steps)]
        low = drives[0]
        for i in range(steps):
            drive[i] = drives[i]
            if i:
                l_hi, l_lo = halves(low)
                low = dot(l_hi, t[i]) + dot(l_lo, t[i]) + drives[i]
        whole[z.width : z.width + z.series, :] = low
        if sender:
            put_chunks(z, by_rows, outs, whole)
        else:
            _, hi, lo, tail = outs
            tail[...] = low
            hi[...], lo[...] = halves(whole[...])

    shapes = [shape(z.buf, z.part)] * z.chunks if sender else [shape(z.tall, z.width), *map_shapes(z)]
    res = call(
        kernel,
        shapes + [jax.ShapeDtypeStruct((steps, z.series, z.width), F32)],
        [transition, gain, observed],
        where,
        scratch=[
            pltpu.VMEM(transition.shape, transition.dtype),
            pltpu.VMEM(gain.shape, gain.dtype),
            pltpu.VMEM(observed.shape, observed.dtype),
            pltpu.SemaphoreType.DMA((3,)),
        ]
        + ([pltpu.VMEM((z.tall, z.width), F32)] if sender else []),
        far=3,
    )
    return (res[:-1], res[-1]) if sender else (res[0], tuple(res[1:4]), res[-1])


def quarter(z, ref, k):
    return ref.at[pl.ds(k * z.buf, z.buf)]


def split_parts(z, refs):
    return [quarter(z, ref, k) for ref in refs for k in range(ref.shape[0] // z.buf)]


def times_chunk(z, where, chunk, own):
    count = chunk.shape[0] // z.buf
    span = count * z.part

    def kernel(by_rows, got, own_hi, own_lo, own_tail, *rest):
        outs, (left, right) = rest[:count], rest[count:]
        gots = split_parts(z, [got])

        @pl.when(by_rows)
        def _():
            left[span:, :] = jnp.zeros((left.shape[0] - span, z.width), F32)
            for j in range(z.chunks):
                cols = slice(j * z.part, (j + 1) * z.part)
                for q, part in enumerate(gots):
                    left[q * z.part : (q + 1) * z.part, cols] = part[j * z.part : (j + 1) * z.part, :]
                left[span : span + z.series, cols] = gots[0][z.width + j * z.series : z.width + (j + 1) * z.series, :]
            l_hi, l_lo = halves(left[...])
            res = dot3(l_hi, l_lo, own_hi[: z.width, :], own_lo[: z.width, :])
            for q, out in enumerate(outs):
                put_rows(z, out, res[q * z.part : (q + 1) * z.part], res[span : span + z.series] + own_tail[...])

        @pl.when(jnp.logical_not(by_rows))
        def _():
            for q, part in enumerate(gots):
                right[:, q * z.part : (q + 1) * z.part] = part[: z.width + z.series, :]
            r_hi, r_lo = halves(right[: z.width, :])
            res = dot3(own_hi[...], own_lo[...], r_hi, r_lo)
            low = res[z.width : z.width + z.series] + right[z.width : z.width + z.series, :]
            for q, out in enumerate(outs):
                cols = slice(q * z.part, (q + 1) * z.part)
                out[z.width :, :] = jnp.zeros((z.buf - z.width, z.part), F32)
                put_cols(z, out, res[: z.width, cols], low[:, cols])

    return call(
        kernel,
        [shape(z.buf, z.part)] * count,
        [chunk, *own],
        where,
        scratch=[pltpu.VMEM((span + z.low, z.width), F32), pltpu.VMEM((z.width + z.series, span), F32)],
    )


def merge(z, where, got, own):
    sent = z.chunks

    def kernel(flag, *refs):
        by_rows, got_left, next_rows = flag
        n = z.chunks
        gots, owns = refs[:n], refs[n : 2 * n]
        outs = split_parts(z, refs[2 * n : 2 * n + sent])
        hi, lo, tail, left_hi, left_lo, left_tail = refs[2 * n + sent : 2 * n + sent + 6]
        a, b, c = refs[2 * n + sent + 6 :]
        clear_low(z, a)
        clear_low(z, b)

        @pl.when(got_left)
        def _():
            gather(z, by_rows, gots, a)
            gather(z, by_rows, owns, b)

        @pl.when(jnp.logical_not(got_left))
        def _():
            gather(z, by_rows, owns, a)
            gather(z, by_rows, gots, b)

        left_hi[...], left_lo[...] = halves(a[...])
        left_tail[...] = a[z.width : z.width + z.series, :]
        r_hi, r_lo = halves(b[: z.width, :])
        c[...] = dot3(left_hi[...], left_lo[...], r_hi, r_lo)
        c[z.width : z.width + z.series, :] = c[z.width : z.width + z.series, :] + b[z.width : z.width + z.series, :]
        put_chunks(z, next_rows, outs, c)
        hi[...], lo[...] = halves(c[...])
        tail[...] = c[z.width : z.width + z.series, :]

    res = call(
        kernel,
        [shape(z.chunks // sent * z.buf, z.part)] * sent + map_shapes(z) * 2,
        list(got) + list(own),
        where,
        scratch=[pltpu.VMEM((z.tall, z.width), F32)] * 3,
    )
    return res[:sent], tuple(res[sent : sent + 3]), tuple(res[sent + 3 :])


def merge_first(z, where, got, own, count):
    span = z.width // count
    n = z.chunks

    def kernel(flag, *refs):
        by_rows, got_left, next_rows = flag
        gots, owns = refs[:n], refs[n : 2 * n]
        out, left_hi, left_lo, left_tail, right_hi, right_lo, right_tail, a, b, c = refs[2 * n :]
        outs = split_parts(z, [out])
        clear_low(z, a)
        clear_low(z, b)

        @pl.when(got_left)
        def _():
            gather(z, by_rows, gots, a)
            gather(z, by_rows, owns, b)

        @pl.when(jnp.logical_not(got_left))
        def _():
            gather(z, by_rows, owns, a)
            gather(z, by_rows, gots, b)

        left_hi[...], left_lo[...] = halves(a[...])
        left_tail[...] = a[z.width : z.width + z.series, :]
        right_hi[...], right_lo[...] = halves(b[...])
        tail = b[z.width : z.width + z.series, :]
        right_tail[...] = tail

        @pl.when(next_rows)
        def _():
            c[:span, :] = a[:span, :]
            c[span : span + z.low, :] = a[z.width :, :]
            c_hi, c_lo = halves(c[: span + z.low, :])
            res = dot3(c_hi, c_lo, right_hi[: z.width, :], right_lo[: z.width, :])
            for q, part in enumerate(outs):
                put_rows(z, part, res[q * z.part : (q + 1) * z.part], res[span : span + z.series] + tail)

        @pl.when(jnp.logical_not(next_rows))
        def _():
            res = dot3(left_hi[...], left_lo[...], right_hi[: z.width, :span], right_lo[: z.width, :span])
            for q, part in enumerate(outs):
                cols = slice(q * z.part, (q + 1) * z.part)
                put_cols(z, part, res[: z.width, cols], res[z.width : z.width + z.series, cols] + tail[:, cols])

    res = call(
        kernel,
        [shape(z.chunks // count * z.buf, z.part)] + map_shapes(z) * 2,
        list(got) + list(own),
        where,
        scratch=[pltpu.VMEM((z.tall, z.width), F32)] * 3,
    )
    return res[0], tuple(res[1:4]), tuple(res[4:7])


def merge_rest(z, where, sent, left, right, count):
    span = z.width // count

    def kernel(flag, *refs):
        next_rows = flag[2]
        done, left_hi, left_lo, _, right_hi, right_lo, right_tail = refs[:7]
        outs = split_parts(z, refs[7 : 6 + count])
        hi, lo, tail, c = refs[6 + count :]
        gather(z, next_rows, split_parts(z, [done]), c)

        @pl.when(next_rows)
        def _():
            c[span:, :] = dot3(left_hi[span:, :], left_lo[span:, :], right_hi[: z.width, :], right_lo[: z.width, :])
            low = c[z.width : z.width + z.series, :] + right_tail[...]
            c[z.width : z.width + z.series, :] = low
            for q, part in enumerate(outs):
                at = span + q * z.part
                put_rows(z, part, c[at : at + z.part, :], low)

        @pl.when(jnp.logical_not(next_rows))
        def _():
            c[z.width + z.series :, :span] = jnp.zeros((z.low - z.series, span), F32)
            c[:, span:] = dot3(left_hi[...], left_lo[...], right_hi[: z.width, span:], right_lo[: z.width, span:])
            low = c[z.width : z.width + z.series, span:] + right_tail[:, span:]
            c[z.width : z.width + z.series, span:] = low
            for q, part in enumerate(outs):
                cols = slice(span + q * z.part, span + (q + 1) * z.part)
                put_cols(z, part, c[: z.width, cols], low[:, q * z.part : (q + 1) * z.part])

        hi[...], lo[...] = halves(c[...])
        tail[...] = c[z.width : z.width + z.series, :]

    res = call(
        kernel,
        [shape(z.chunks // count * z.buf, z.part)] * (count - 1) + map_shapes(z),
        [sent, *left, *right],
        where,
        scratch=[pltpu.VMEM((z.tall, z.width), F32)],
    )
    return [sent, *res[: count - 1]], tuple(res[count - 1 :])


def assemble(z, where, chunks, others=None, with_tail=True):
    extra = [] if others is None else list(others)

    def kernel(flag, *refs):
        by_rows, swap = flag
        n = len(chunks)
        bufs, rest = split_parts(z, refs[:n]), refs[n : n + len(extra)]
        hi, lo, *tail, full = refs[n + len(extra) :]
        clear_low(z, full)
        if not extra:
            gather(z, by_rows, bufs, full)
        else:

            @pl.when(jnp.logical_not(swap))
            def _():
                gather(z, by_rows, bufs, full)

            @pl.when(swap)
            def _():
                if len(rest) == 1:
                    full[...] = rest[0][...]
                else:
                    gather(z, by_rows, rest, full)

        hi[...], lo[...] = halves(full[...])
        if with_tail:
            tail[0][...] = full[z.width : z.width + z.series, :]

    return call(
        kernel,
        map_shapes(z) if with_tail else map_shapes(z)[:2],
        list(chunks) + extra,
        where,
        scratch=[pltpu.VMEM((z.tall, z.width), F32)],
    )


def padded(series):
    return 8 * (-(-series // 8))


def advance(z, where, parts, block, before=None, split=False):
    rows = sum(p.shape[0] for p in parts)
    operands = list(parts) + list(block[:2]) + ([] if before is None else [before])
    m = len(parts)

    def kernel(active, *refs):
        given, (hi, lo), outs = refs[:m], refs[m : m + 2], refs[len(operands) :]

        def put(value):
            for i, out in enumerate(outs):
                out[...] = value[i * out.shape[0] : (i + 1) * out.shape[0]]

        def run():
            state = given[0][...] if m == 1 else jnp.concatenate([g[...] for g in given])
            put(few(state, hi[: z.width, :], lo[: z.width, :]))

        pl.when(active)(run)
        if before is not None:

            @pl.when(jnp.logical_not(active))
            def _():
                put(refs[m + 2][...])

    outs = [shape(rows // 2, z.width)] * 2 if split else [shape(rows, z.width)]
    res = call(kernel, outs, operands, where)
    return res if split else res[0]


def advance_mean(z, mean, block):
    low = padded(z.series)

    def kernel(given, hi, lo, tail, out):
        now = given[...]
        if given.shape[0] < low:
            now = jnp.concatenate([now, jnp.zeros((low - given.shape[0], z.width), F32)])
        out[...] = few(now, hi[: z.width, :], lo[: z.width, :])
        out[: z.series, :] = out[: z.series, :] + tail[...]

    return call(kernel, shape(low, z.width), [mean, *block])


def deal(where, kept, got):
    def kernel(received, a, b, out):
        @pl.when(received)
        def _():
            out[0] = b[...]

        @pl.when(jnp.logical_not(received))
        def _():
            out[0] = a[...]

    return call(kernel, jax.ShapeDtypeStruct((1, *kept.shape), F32), [kept, got], where)


def load_choice(z, index, refs, into):
    for i, ref in enumerate(refs):

        @pl.when(index == i)
        def _():
            if ref.shape[0] == z.series:
                into[...] = jnp.zeros(into.shape, F32)
                into[: z.series, :] = ref[...]
            else:
                into[...] = ref[ref.shape[0] - into.shape[0] :, :]


def descend(z, where, candidates, left, cross=None):
    low = padded(z.series)
    m = len(candidates)
    maps = list(left) + ([] if cross is None else list(cross))

    def kernel(flag, *refs):
        index, through, in_right = flag
        hi, lo, tail = refs[m : m + 3]
        mine, other, now = refs[m + len(maps) :]
        load_choice(z, index, refs[:m], now)
        if cross is not None:

            @pl.when(through)
            def _():
                c_hi, c_lo, c_tail = refs[m + 3 : m + 6]
                now[...] = few(now[...], c_hi[: z.width, :], c_lo[: z.width, :])
                now[: z.series, :] = now[: z.series, :] + c_tail[...]

        beyond = few(now[...], hi[: z.width, :], lo[: z.width, :])

        @pl.when(in_right)
        def _():
            mine[...] = beyond
            mine[: z.series, :] = mine[: z.series, :] + tail[...]
            other[...] = now[...]

        @pl.when(jnp.logical_not(in_right))
        def _():
            other[...] = beyond
            other[: z.series, :] = other[: z.series, :] + tail[...]
            mine[...] = now[...]

    return call(
        kernel, [shape(low, z.width)] * 2, [*candidates, *maps], where, scratch=[pltpu.VMEM((low, z.width), F32)]
    )


def last_steps(z, where, candidates, left, transition, drives):
    steps = transition.shape[0]
    m = len(candidates)
    low = padded(z.series)

    def kernel(flag, *refs):
        index, through, second = flag
        hi, lo, tail, t, d0, d1, out, now = refs[m:]
        load_choice(z, index, refs[:m], now)

        @pl.when(through)
        def _():
            now[...] = few(now[...], hi[: z.width, :], lo[: z.width, :])
            now[: z.series, :] = now[: z.series, :] + tail[...]

        for i in range(steps):
            now[...] = few(now[...], t[i])
            now[: z.series, :] = now[: z.series, :] + jnp.where(second, d1[i], d0[i])
            out[i] = now[: z.series, :]

    return call(
        kernel,
        jax.ShapeDtypeStruct((steps, z.series, z.width), F32),
        [*candidates, *left, transition, *drives],
        where,
        scratch=[pltpu.VMEM((low, z.width), F32)],
    )


class Tree:
    def __init__(self, segs, size):
        self.segs, self.size = segs, size
        self.depth = size.bit_length() - 1
        if size != 1 << self.depth or self.depth < 3:
            raise ValueError("tm size")

    def root(self, odd, level, group):
        if level == 1:
            return 2 * group + (0 if odd else 1)
        return self.root(odd, level - 1, 2 * group + (1 - group % 2))

    def pairs(self, per_parity):
        return [
            (s * self.size + a, s * self.size + b) for s in range(self.segs) for a, b in per_parity(s % 2)
        ]

    def child_roots(self, odd, level, group):
        return self.root(odd, level - 1, 2 * group), self.root(odd, level - 1, 2 * group + 1)

    def up(self, level):
        def of(odd):
            if level == 1:
                return [(i, i ^ 1) for i in range(self.size) if i % 2 == (1 if odd else 0)]
            found = []
            for g in range(self.size >> level):
                a, b = self.child_roots(odd, level, g)
                if level == self.depth:
                    found += [(a, b), (b, a)]
                else:
                    found.append((a, b) if g % 2 == 0 else (b, a))
            return found

        return self.pairs(of)

    def far(self, bit, seg=None):
        found = []
        for s in range(self.segs) if seg is None else [seg]:
            for i in range(self.size):
                away = i // 2 ^ self.root(0, self.depth - 1, 2 * i // self.size) // 2
                if bit <= away < 2 * bit:
                    found.append((s * self.size + i, s * self.size + (i ^ 2 * bit)))
        return found

    def holds(self, i):
        return i // 2 == self.root(0, self.depth - 1, 2 * i // self.size) // 2

    def root_of(self, odd, level, group):
        for _ in range(level - 1):
            group = 2 * group + 1 - group % 2
        return 2 * group + 1 - odd


def tied(x, after):
    return lax.optimization_barrier((x, after))[0]


def make(mesh):
    segs, size = mesh.shape["seg"], mesh.shape["tm"]
    tree = Tree(segs, size)
    depth = tree.depth
    half = size // 2

    def send(x, pairs):
        return lax.ppermute(x, AXES, pairs)

    def others(level, flip):
        def of(odd):
            found = []
            for g in range(size >> level):
                root = tree.root(odd, level, g)
                a, b = tree.child_roots(odd, level, g)
                found.append((root, (a if root == b else b) ^ flip))
            return found

        return tree.pairs(of)

    def top_and_other(seg, tm, level):
        odd, group = seg % 2, tm >> level
        top = tree.root_of(odd, level, group)
        a, b = (tree.root_of(odd, level - 1, 2 * group + i) for i in (0, 1))
        return top, a + b - top

    def per_device(transition, obs_gain, observed, init_mean, init_factor):
        width, series = transition.shape[1], observed.shape[1]
        chunks = next(n for n in (4, 2, 1) if width % (n * 128) == 0 or n == 1)
        z = Sizes(width, series, chunks)

        def is_even(seg, tm):
            return seg % 2 == 0

        def in_right_half(seg, tm):
            return tm >= half

        def sends(seg, tm):
            return seg % 2 == 0, (seg + tm) % 2 == 0

        def receives(seg, tm):
            return seg % 2 == 0, (seg + tm) % 2 == 1

        def one_chunk(c):
            return times_chunk(z, is_even, c, own_map)[0]

        own, early = local_map(z, sends, transition, obs_gain, observed, True)
        first = [send(c, tree.up(1)) for c in own]
        whole, own_map, late = local_map(z, receives, transition, obs_gain, observed, False)
        outs = [one_chunk(c) for c in first]
        back = send(tied(whole, outs), tree.pairs(lambda odd: [(i, i + 1) for i in range(0, size, 2)] if odd else []))
        bits = [1 << i for i in range(depth - 3, -1, -1)]
        start = [init_factor]
        for bit in bits:
            held = start[0] if len(start) == 1 else jnp.concatenate(start)
            start = [held, send(tied(held, outs), tree.far(bit, 0))]
        lefts = {}
        for level in range(2, depth):

            def where(seg, tm, level=level):
                by_rows = seg % 2 == 0 if level == 2 else seg >= 0
                next_rows = tm < half if level == depth - 1 else seg >= 0
                return by_rows, (tm >> level) % 2 == 0, next_rows

            got = [send(c, tree.up(level)) for c in outs]
            if level < depth - 1 or chunks == 1:
                outs, mine, lefts[level] = merge(z, where, got, outs)
            else:
                sent, lefts[level], right = merge_first(z, where, got, outs, 2)
                outs, mine = merge_rest(z, where, sent, lefts[level], right, 2)
        crossed = [send(c, tree.up(depth)) for c in outs]
        final = [part for c in crossed for part in times_chunk(z, in_right_half, c, mine)]
        a, b = tree.child_roots(0, depth, 0)
        halved = send(advance_mean(z, init_mean, mine), [(a, b)])
        onward = advance_mean(z, halved, mine)
        nexts = [(b, size + r) for r in tree.child_roots(1, depth, 0)]
        second = send(onward, nexts[1:]) + send(onward, nexts[:1])
        roots = tree.pairs(lambda odd: [(r, r ^ 1) for r in tree.child_roots(odd, depth, 0)])
        got = [send(c, roots) for c in final]
        left = assemble(z, lambda seg, tm: (seg >= 0, seg % 2 == 1), first, [back])
        halfway = assemble(z, lambda seg, tm: (seg >= 0, seg < 0), crossed)
        got[-1], left, halfway = lax.optimization_barrier((got[-1], left, halfway))

        def beside(seg, tm):
            return tm >= half, tm ^ 1 == tree.root_of(seg % 2, depth - 1, tm // half)

        block = assemble(z, beside, final, got, with_tail=False)

        at_root = assemble(z, lambda seg, tm: (tm >= half, seg < 0), final)
        entries = [init_mean, second]
        for turn in range(2, segs):
            pairs = []
            for h in (0, 1):
                a, b = (tree.root(s % 2, depth - 1, h) for s in (turn - 1, turn))
                pairs.append(((turn - 1) * size + a, turn * size + b))
            gone = advance_mean(z, entries[-1], at_root)
            entries.append(send(gone, pairs))

        moved = advance(z, lambda seg, tm: seg == 0, start, block)
        for turn in range(1, segs):
            pairs = [((turn - 1) * size + i, turn * size + i) for i in range(size) if tree.holds(i)]
            arrived = send(moved, pairs)

            def where(seg, tm, turn=turn):
                return seg >= turn

            moved = advance(z, where, [arrived], block, moved, turn == segs - 1)

        def down(arrivals):
            candidates, cross = arrivals, halfway
            for level in range(depth - 1, 1, -1):

                def where(seg, tm, level=level):
                    if level == depth - 1:
                        index = seg
                    else:
                        index = (tm == top_and_other(seg, tm, level + 1)[1]).astype(jnp.int32)
                    return index, tm >= half, (tm >> level) % 2 == 0

                mine_in, other_in = descend(z, where, candidates, lefts[level], cross)
                candidates, cross = [mine_in, send(other_in, others(level, 0))], None
            near = tree.pairs(lambda odd: [(tree.root(odd, 2, g), tree.root(odd, 2, g) ^ 1) for g in range(size >> 2)])
            return [*candidates, send(other_in, others(2, 1)), send(mine_in, near)]

        candidates = down(entries)

        kept, given = moved
        for bit in reversed(bits):
            back_pairs = [(b, a) for a, b in tree.far(bit)]
            came = send(given, back_pairs)

            def where(seg, tm, bit=bit):
                away = tm // 2 ^ tree.root_of(0, depth - 1, tm // half) // 2
                return (away >= bit) & (away < 2 * bit)

            kept = deal(where, kept, came)
            if bit != bits[0]:
                rows = kept.shape[1] // 2
                kept, given = kept[0, :rows], kept[0, rows:]
        ends = kept

        def where(seg, tm):
            top, other = top_and_other(seg, tm, 2)
            index = jnp.where(tm == other, 1, jnp.where(tm == other ^ 1, 2, jnp.where(tm == top, 0, 3)))
            return index, tm % 2 == 1, (seg + tm) % 2 == 1

        return last_steps(z, where, candidates, left, transition, (early, late)), ends

    return per_device


def solution(mesh):
    return jax.shard_map(
        make(mesh),
        mesh=mesh,
        in_specs=(
            P(("seg", "tm"), None, None),
            P(("seg", "tm"), None, None),
            P(("seg", "tm"), None, None),
            P(),
            P("tm", None),
        ),
        out_specs=(P(("seg", "tm"), None, None), P("seg", "tm", None)),
        check_vma=False,
    )
```

```python
import jax
import jax.numpy as jnp
from jax import lax
from jax.experimental import pallas as pl
from jax.experimental.pallas import tpu as pltpu
from jax.sharding import PartitionSpec as P

F32 = jnp.float32
BF16 = jnp.bfloat16
AXES = ("seg", "tm")
GRANT = 10 * 1024 * 1024


def halves(x):
    hi = x.astype(BF16)
    return hi, (x - hi.astype(F32)).astype(BF16)


def dot(a, b):
    return jnp.dot(a, b, preferred_element_type=F32)


def dot3(a_hi, a_lo, b_hi, b_lo):
    return dot(a_hi, b_hi) + (dot(a_hi, b_lo) + dot(a_lo, b_hi))


def few(rows, hi, lo=None):
    r_hi = rows.astype(BF16)
    r_hi32 = r_hi.astype(F32)
    both = jnp.concatenate([r_hi32, rows - r_hi32]).astype(BF16)
    res = dot(both, hi)
    res = res[: rows.shape[0]] + res[rows.shape[0] :]
    return res if lo is None else res + dot(r_hi, lo)


class Sizes:
    def __init__(self, width, series, chunks):
        self.width, self.series, self.chunks = width, series, chunks
        self.part = width // chunks
        self.tall = width + 16 * (-(-series // 16))
        self.buf = width + 8 * (-(-chunks * series // 8))
        self.low = self.tall - width


def put_rows(z, out, body, tail):
    for j in range(z.chunks):
        cols = slice(j * z.part, (j + 1) * z.part)
        out[j * z.part : (j + 1) * z.part, :] = body[:, cols]
        out[z.width + j * z.series : z.width + (j + 1) * z.series, :] = tail[:, cols]


def put_cols(z, out, body, tail):
    out[: z.width, :] = body
    out[z.width : z.width + z.series, :] = tail


def gather_rows(z, bufs, full):
    for k, buf in enumerate(bufs):
        for j in range(z.chunks):
            full[k * z.part : (k + 1) * z.part, j * z.part : (j + 1) * z.part] = buf[j * z.part : (j + 1) * z.part, :]
    for j in range(z.chunks):
        full[z.width : z.width + z.series, j * z.part : (j + 1) * z.part] = bufs[0][
            z.width + j * z.series : z.width + (j + 1) * z.series, :
        ]


def gather_cols(z, bufs, full):
    for k, buf in enumerate(bufs):
        cols = slice(k * z.part, (k + 1) * z.part)
        full[: z.width, cols] = buf[: z.width, :]
        full[z.width : z.width + z.series, cols] = buf[z.width : z.width + z.series, :]


def clear_low(z, full):
    full[z.width :, :] = jnp.zeros((z.low, z.width), F32)


def put_chunks(z, by_rows, outs, full):
    @pl.when(by_rows)
    def _():
        for k, out in enumerate(outs):
            put_rows(z, out, full[k * z.part : (k + 1) * z.part, :], full[z.width : z.width + z.series, :])

    @pl.when(jnp.logical_not(by_rows))
    def _():
        for k, out in enumerate(outs):
            cols = slice(k * z.part, (k + 1) * z.part)
            put_cols(z, out, full[: z.width, cols], full[z.width : z.width + z.series, cols])


def call(kernel, outs, operands, where=None, scratch=(), far=0):
    in_specs = [pl.BlockSpec(memory_space=pltpu.HBM if i < far else pltpu.VMEM) for i in range(len(operands))]
    operands = [pltpu.with_memory_space_constraint(x, pltpu.HBM) if i < far else x for i, x in enumerate(operands)]

    def body(*refs):
        if where is None:
            kernel(*refs)
        else:
            kernel(where(lax.axis_index("seg"), lax.axis_index("tm")), *refs)

    return pl.pallas_call(
        body,
        out_shape=outs,
        in_specs=in_specs,
        out_specs=jax.tree.map(lambda _: pl.BlockSpec(memory_space=pltpu.VMEM), outs),
        scratch_shapes=list(scratch),
        compiler_params=pltpu.CompilerParams(vmem_limit_bytes=GRANT),
    )(*operands)


def shape(rows, cols, dtype=F32):
    return jax.ShapeDtypeStruct((rows, cols), dtype)


def gather(z, by_rows, bufs, full):
    @pl.when(by_rows)
    def _():
        gather_rows(z, bufs, full)

    @pl.when(jnp.logical_not(by_rows))
    def _():
        gather_cols(z, bufs, full)


def map_shapes(z):
    return [shape(z.tall, z.width, BF16), shape(z.tall, z.width, BF16), shape(z.series, z.width)]


def local_map(z, where, transition, gain, observed, sender):
    steps = transition.shape[0]
    count = z.chunks if sender else 4

    def kernel(flag, *refs):
        by_rows, active = flag
        pl.when(active)(lambda: run(by_rows, *refs))

    def run(by_rows, t_hbm, g_hbm, o_hbm, *rest):
        outs, drive, t, g, o, sems = rest[:count], *rest[count : count + 5]
        whole = rest[-1] if sender else outs[0]
        copies = [
            pltpu.make_async_copy(t_hbm, t, sems.at[0]),
            pltpu.make_async_copy(g_hbm, g, sems.at[1]),
            pltpu.make_async_copy(o_hbm, o, sems.at[2]),
        ]
        for copy in copies:
            copy.start()
        copies[0].wait()
        body = t[0]
        for i in range(1, steps):
            if i == 1:
                body = dot(body, t[i])
            else:
                b_hi, b_lo = halves(body)
                body = dot(b_hi, t[i]) + dot(b_lo, t[i])
        clear_low(z, whole)
        whole[: z.width, :] = body.astype(F32)
        copies[1].wait()
        copies[2].wait()
        drives = [dot(o[i], g[i]) for i in range(steps)]
        low = drives[0]
        for i in range(steps):
            drive[i] = drives[i]
            if i:
                l_hi, l_lo = halves(low)
                low = dot(l_hi, t[i]) + dot(l_lo, t[i]) + drives[i]
        whole[z.width : z.width + z.series, :] = low
        if sender:
            put_chunks(z, by_rows, outs, whole)
        else:
            _, hi, lo, tail = outs
            tail[...] = low
            hi[...], lo[...] = halves(whole[...])

    shapes = [shape(z.buf, z.part)] * z.chunks if sender else [shape(z.tall, z.width), *map_shapes(z)]
    res = call(
        kernel,
        shapes + [jax.ShapeDtypeStruct((steps, z.series, z.width), F32)],
        [transition, gain, observed],
        where,
        scratch=[
            pltpu.VMEM(transition.shape, transition.dtype),
            pltpu.VMEM(gain.shape, gain.dtype),
            pltpu.VMEM(observed.shape, observed.dtype),
            pltpu.SemaphoreType.DMA((3,)),
        ]
        + ([pltpu.VMEM((z.tall, z.width), F32)] if sender else []),
        far=3,
    )
    return (res[:-1], res[-1]) if sender else (res[0], tuple(res[1:4]), res[-1])


def quarter(z, ref, k):
    return ref.at[pl.ds(k * z.buf, z.buf)]


def split_parts(z, refs):
    return [quarter(z, ref, k) for ref in refs for k in range(ref.shape[0] // z.buf)]


def times_chunk(z, where, chunk, own):
    count = chunk.shape[0] // z.buf
    span = count * z.part

    def kernel(by_rows, got, own_hi, own_lo, own_tail, *rest):
        outs, (left, right) = rest[:count], rest[count:]
        gots = split_parts(z, [got])

        @pl.when(by_rows)
        def _():
            left[span:, :] = jnp.zeros((left.shape[0] - span, z.width), F32)
            for j in range(z.chunks):
                cols = slice(j * z.part, (j + 1) * z.part)
                for q, part in enumerate(gots):
                    left[q * z.part : (q + 1) * z.part, cols] = part[j * z.part : (j + 1) * z.part, :]
                left[span : span + z.series, cols] = gots[0][z.width + j * z.series : z.width + (j + 1) * z.series, :]
            l_hi, l_lo = halves(left[...])
            res = dot3(l_hi, l_lo, own_hi[: z.width, :], own_lo[: z.width, :])
            for q, out in enumerate(outs):
                put_rows(z, out, res[q * z.part : (q + 1) * z.part], res[span : span + z.series] + own_tail[...])

        @pl.when(jnp.logical_not(by_rows))
        def _():
            for q, part in enumerate(gots):
                right[:, q * z.part : (q + 1) * z.part] = part[: z.width + z.series, :]
            r_hi, r_lo = halves(right[: z.width, :])
            res = dot3(own_hi[...], own_lo[...], r_hi, r_lo)
            low = res[z.width : z.width + z.series] + right[z.width : z.width + z.series, :]
            for q, out in enumerate(outs):
                cols = slice(q * z.part, (q + 1) * z.part)
                out[z.width :, :] = jnp.zeros((z.buf - z.width, z.part), F32)
                put_cols(z, out, res[: z.width, cols], low[:, cols])

    return call(
        kernel,
        [shape(z.buf, z.part)] * count,
        [chunk, *own],
        where,
        scratch=[pltpu.VMEM((span + z.low, z.width), F32), pltpu.VMEM((z.width + z.series, span), F32)],
    )


def merge(z, where, got, own):
    sent = z.chunks

    def kernel(flag, *refs):
        by_rows, got_left, next_rows = flag
        n = z.chunks
        gots, owns = refs[:n], refs[n : 2 * n]
        outs = split_parts(z, refs[2 * n : 2 * n + sent])
        hi, lo, tail, left_hi, left_lo, left_tail = refs[2 * n + sent : 2 * n + sent + 6]
        a, b, c = refs[2 * n + sent + 6 :]
        clear_low(z, a)
        clear_low(z, b)

        @pl.when(got_left)
        def _():
            gather(z, by_rows, gots, a)
            gather(z, by_rows, owns, b)

        @pl.when(jnp.logical_not(got_left))
        def _():
            gather(z, by_rows, owns, a)
            gather(z, by_rows, gots, b)

        left_hi[...], left_lo[...] = halves(a[...])
        left_tail[...] = a[z.width : z.width + z.series, :]
        r_hi, r_lo = halves(b[: z.width, :])
        c[...] = dot3(left_hi[...], left_lo[...], r_hi, r_lo)
        c[z.width : z.width + z.series, :] = c[z.width : z.width + z.series, :] + b[z.width : z.width + z.series, :]
        put_chunks(z, next_rows, outs, c)
        hi[...], lo[...] = halves(c[...])
        tail[...] = c[z.width : z.width + z.series, :]

    res = call(
        kernel,
        [shape(z.chunks // sent * z.buf, z.part)] * sent + map_shapes(z) * 2,
        list(got) + list(own),
        where,
        scratch=[pltpu.VMEM((z.tall, z.width), F32)] * 3,
    )
    return res[:sent], tuple(res[sent : sent + 3]), tuple(res[sent + 3 :])


def merge_first(z, where, got, own, count):
    span = z.width // count
    n = z.chunks

    def kernel(flag, *refs):
        by_rows, got_left, next_rows = flag
        gots, owns = refs[:n], refs[n : 2 * n]
        out, left_hi, left_lo, left_tail, right_hi, right_lo, right_tail, a, b, c = refs[2 * n :]
        outs = split_parts(z, [out])
        clear_low(z, a)
        clear_low(z, b)

        @pl.when(got_left)
        def _():
            gather(z, by_rows, gots, a)
            gather(z, by_rows, owns, b)

        @pl.when(jnp.logical_not(got_left))
        def _():
            gather(z, by_rows, owns, a)
            gather(z, by_rows, gots, b)

        left_hi[...], left_lo[...] = halves(a[...])
        left_tail[...] = a[z.width : z.width + z.series, :]
        right_hi[...], right_lo[...] = halves(b[...])
        tail = b[z.width : z.width + z.series, :]
        right_tail[...] = tail

        @pl.when(next_rows)
        def _():
            c[:span, :] = a[:span, :]
            c[span : span + z.low, :] = a[z.width :, :]
            c_hi, c_lo = halves(c[: span + z.low, :])
            res = dot3(c_hi, c_lo, right_hi[: z.width, :], right_lo[: z.width, :])
            for q, part in enumerate(outs):
                put_rows(z, part, res[q * z.part : (q + 1) * z.part], res[span : span + z.series] + tail)

        @pl.when(jnp.logical_not(next_rows))
        def _():
            res = dot3(left_hi[...], left_lo[...], right_hi[: z.width, :span], right_lo[: z.width, :span])
            for q, part in enumerate(outs):
                cols = slice(q * z.part, (q + 1) * z.part)
                put_cols(z, part, res[: z.width, cols], res[z.width : z.width + z.series, cols] + tail[:, cols])

    res = call(
        kernel,
        [shape(z.chunks // count * z.buf, z.part)] + map_shapes(z) * 2,
        list(got) + list(own),
        where,
        scratch=[pltpu.VMEM((z.tall, z.width), F32)] * 3,
    )
    return res[0], tuple(res[1:4]), tuple(res[4:7])


def merge_rest(z, where, sent, left, right, count):
    span = z.width // count

    def kernel(flag, *refs):
        next_rows = flag[2]
        done, left_hi, left_lo, _, right_hi, right_lo, right_tail = refs[:7]
        outs = split_parts(z, refs[7 : 6 + count])
        hi, lo, tail, c = refs[6 + count :]
        gather(z, next_rows, split_parts(z, [done]), c)

        @pl.when(next_rows)
        def _():
            c[span:, :] = dot3(left_hi[span:, :], left_lo[span:, :], right_hi[: z.width, :], right_lo[: z.width, :])
            low = c[z.width : z.width + z.series, :] + right_tail[...]
            c[z.width : z.width + z.series, :] = low
            for q, part in enumerate(outs):
                at = span + q * z.part
                put_rows(z, part, c[at : at + z.part, :], low)

        @pl.when(jnp.logical_not(next_rows))
        def _():
            c[z.width + z.series :, :span] = jnp.zeros((z.low - z.series, span), F32)
            c[:, span:] = dot3(left_hi[...], left_lo[...], right_hi[: z.width, span:], right_lo[: z.width, span:])
            low = c[z.width : z.width + z.series, span:] + right_tail[:, span:]
            c[z.width : z.width + z.series, span:] = low
            for q, part in enumerate(outs):
                cols = slice(span + q * z.part, span + (q + 1) * z.part)
                put_cols(z, part, c[: z.width, cols], low[:, q * z.part : (q + 1) * z.part])

        hi[...], lo[...] = halves(c[...])
        tail[...] = c[z.width : z.width + z.series, :]

    res = call(
        kernel,
        [shape(z.chunks // count * z.buf, z.part)] * (count - 1) + map_shapes(z),
        [sent, *left, *right],
        where,
        scratch=[pltpu.VMEM((z.tall, z.width), F32)],
    )
    return [sent, *res[: count - 1]], tuple(res[count - 1 :])


def assemble(z, where, chunks, others=None, with_tail=True):
    extra = [] if others is None else list(others)

    def kernel(flag, *refs):
        by_rows, swap = flag
        n = len(chunks)
        bufs, rest = split_parts(z, refs[:n]), refs[n : n + len(extra)]
        hi, lo, *tail, full = refs[n + len(extra) :]
        clear_low(z, full)
        if not extra:
            gather(z, by_rows, bufs, full)
        else:

            @pl.when(jnp.logical_not(swap))
            def _():
                gather(z, by_rows, bufs, full)

            @pl.when(swap)
            def _():
                if len(rest) == 1:
                    full[...] = rest[0][...]
                else:
                    gather(z, by_rows, rest, full)

        hi[...], lo[...] = halves(full[...])
        if with_tail:
            tail[0][...] = full[z.width : z.width + z.series, :]

    return call(
        kernel,
        map_shapes(z) if with_tail else map_shapes(z)[:2],
        list(chunks) + extra,
        where,
        scratch=[pltpu.VMEM((z.tall, z.width), F32)],
    )


def padded(series):
    return 8 * (-(-series // 8))


def advance(z, where, parts, block, before=None, split=False):
    rows = sum(p.shape[0] for p in parts)
    operands = list(parts) + list(block[:2]) + ([] if before is None else [before])
    m = len(parts)

    def kernel(active, *refs):
        given, (hi, lo), outs = refs[:m], refs[m : m + 2], refs[len(operands) :]

        def put(value):
            for i, out in enumerate(outs):
                out[...] = value[i * out.shape[0] : (i + 1) * out.shape[0]]

        def run():
            state = given[0][...] if m == 1 else jnp.concatenate([g[...] for g in given])
            put(few(state, hi[: z.width, :], lo[: z.width, :]))

        pl.when(active)(run)
        if before is not None:

            @pl.when(jnp.logical_not(active))
            def _():
                put(refs[m + 2][...])

    outs = [shape(rows // 2, z.width)] * 2 if split else [shape(rows, z.width)]
    res = call(kernel, outs, operands, where)
    return res if split else res[0]


def pick(where, one, two):
    def kernel(flag, a, b, out):
        @pl.when(flag)
        def _():
            out[...] = a[...]

        @pl.when(jnp.logical_not(flag))
        def _():
            out[...] = b[...]

    return call(kernel, shape(*one.shape), [one, two], where)


def advance_mean(z, mean, block):
    low = padded(z.series)

    def kernel(given, hi, lo, tail, out):
        now = given[...]
        if given.shape[0] < low:
            now = jnp.concatenate([now, jnp.zeros((low - given.shape[0], z.width), F32)])
        out[...] = few(now, hi[: z.width, :], lo[: z.width, :])
        out[: z.series, :] = out[: z.series, :] + tail[...]

    return call(kernel, shape(low, z.width), [mean, *block])


def deal(where, kept, got):
    def kernel(received, a, b, out):
        @pl.when(received)
        def _():
            out[0] = b[...]

        @pl.when(jnp.logical_not(received))
        def _():
            out[0] = a[...]

    return call(kernel, jax.ShapeDtypeStruct((1, *kept.shape), F32), [kept, got], where)


def load_choice(z, index, refs, into):
    for i, ref in enumerate(refs):

        @pl.when(index == i)
        def _():
            if ref.shape[0] == z.series:
                into[...] = jnp.zeros(into.shape, F32)
                into[: z.series, :] = ref[...]
            else:
                into[...] = ref[ref.shape[0] - into.shape[0] :, :]


def descend(z, where, candidates, left, cross=None):
    low = padded(z.series)
    m = len(candidates)
    maps = list(left) + ([] if cross is None else list(cross))

    def kernel(flag, *refs):
        index, through, in_right = flag
        hi, lo, tail = refs[m : m + 3]
        mine, other, now = refs[m + len(maps) :]
        load_choice(z, index, refs[:m], now)
        if cross is not None:

            @pl.when(through)
            def _():
                c_hi, c_lo, c_tail = refs[m + 3 : m + 6]
                now[...] = few(now[...], c_hi[: z.width, :], c_lo[: z.width, :])
                now[: z.series, :] = now[: z.series, :] + c_tail[...]

        beyond = few(now[...], hi[: z.width, :], lo[: z.width, :])

        @pl.when(in_right)
        def _():
            mine[...] = beyond
            mine[: z.series, :] = mine[: z.series, :] + tail[...]
            other[...] = now[...]

        @pl.when(jnp.logical_not(in_right))
        def _():
            other[...] = beyond
            other[: z.series, :] = other[: z.series, :] + tail[...]
            mine[...] = now[...]

    return call(
        kernel, [shape(low, z.width)] * 2, [*candidates, *maps], where, scratch=[pltpu.VMEM((low, z.width), F32)]
    )


def last_steps(z, where, candidates, left, transition, drives):
    steps = transition.shape[0]
    m = len(candidates)
    low = padded(z.series)

    def kernel(flag, *refs):
        index, through, second = flag
        hi, lo, tail, t, d0, d1, out, now = refs[m:]
        load_choice(z, index, refs[:m], now)

        @pl.when(through)
        def _():
            now[...] = few(now[...], hi[: z.width, :], lo[: z.width, :])
            now[: z.series, :] = now[: z.series, :] + tail[...]

        for i in range(steps):
            now[...] = few(now[...], t[i])
            now[: z.series, :] = now[: z.series, :] + jnp.where(second, d1[i], d0[i])
            out[i] = now[: z.series, :]

    return call(
        kernel,
        jax.ShapeDtypeStruct((steps, z.series, z.width), F32),
        [*candidates, *left, transition, *drives],
        where,
        scratch=[pltpu.VMEM((low, z.width), F32)],
    )


class Tree:
    def __init__(self, segs, size):
        self.segs, self.size = segs, size
        self.depth = size.bit_length() - 1
        if size != 1 << self.depth or self.depth < 3:
            raise ValueError("tm size")

    def root(self, odd, level, group):
        if level == 1:
            return 2 * group + (0 if odd else 1)
        return self.root(odd, level - 1, 2 * group + (1 - group % 2))

    def pairs(self, per_parity):
        return [
            (s * self.size + a, s * self.size + b) for s in range(self.segs) for a, b in per_parity(s % 2)
        ]

    def child_roots(self, odd, level, group):
        return self.root(odd, level - 1, 2 * group), self.root(odd, level - 1, 2 * group + 1)

    def up(self, level):
        def of(odd):
            if level == 1:
                return [(i, i ^ 1) for i in range(self.size) if i % 2 == (1 if odd else 0)]
            found = []
            for g in range(self.size >> level):
                a, b = self.child_roots(odd, level, g)
                if level == self.depth:
                    found += [(a, b), (b, a)]
                else:
                    found.append((a, b) if g % 2 == 0 else (b, a))
            return found

        return self.pairs(of)

    def far(self, bit, seg=None):
        found = []
        for s in range(self.segs) if seg is None else [seg]:
            for i in range(self.size):
                away = i // 2 ^ self.root(0, self.depth - 1, 2 * i // self.size) // 2
                if bit <= away < 2 * bit:
                    found.append((s * self.size + i, s * self.size + (i ^ 2 * bit)))
        return found

    def holds(self, i):
        return i // 2 == self.root(0, self.depth - 1, 2 * i // self.size) // 2

    def root_of(self, odd, level, group):
        for _ in range(level - 1):
            group = 2 * group + 1 - group % 2
        return 2 * group + 1 - odd


def tied(x, after):
    return lax.optimization_barrier((x, after))[0]


def make(mesh):
    segs, size = mesh.shape["seg"], mesh.shape["tm"]
    tree = Tree(segs, size)
    depth = tree.depth
    half = size // 2

    def send(x, pairs):
        return lax.ppermute(x, AXES, pairs)

    def others(level, flip):
        def of(odd):
            found = []
            for g in range(size >> level):
                root = tree.root(odd, level, g)
                a, b = tree.child_roots(odd, level, g)
                found.append((root, (a if root == b else b) ^ flip))
            return found

        return tree.pairs(of)

    def top_and_other(seg, tm, level):
        odd, group = seg % 2, tm >> level
        top = tree.root_of(odd, level, group)
        a, b = (tree.root_of(odd, level - 1, 2 * group + i) for i in (0, 1))
        return top, a + b - top

    def per_device(transition, obs_gain, observed, init_mean, init_factor):
        width, series = transition.shape[1], observed.shape[1]
        chunks = next(n for n in (4, 2, 1) if width % (n * 128) == 0 or n == 1)
        z = Sizes(width, series, chunks)

        def is_even(seg, tm):
            return seg % 2 == 0

        def in_right_half(seg, tm):
            return tm >= half

        def sends(seg, tm):
            return seg % 2 == 0, (seg + tm) % 2 == 0

        def receives(seg, tm):
            return seg % 2 == 0, (seg + tm) % 2 == 1

        def one_chunk(c):
            return times_chunk(z, is_even, c, own_map)[0]

        own, early = local_map(z, sends, transition, obs_gain, observed, True)
        first = [send(c, tree.up(1)) for c in own]
        whole, own_map, late = local_map(z, receives, transition, obs_gain, observed, False)
        outs = [one_chunk(c) for c in first]
        back = send(tied(whole, outs), tree.pairs(lambda odd: [(i, i + 1) for i in range(0, size, 2)] if odd else []))
        order, bits = [0], [1 << i for i in range(depth - 3, -1, -1)]
        for bit in bits:
            order += [o ^ bit for o in order]
        rows_in = tied(init_factor, outs)
        start = []
        for away in [2 * o for o in order] + [2 * o ^ 1 for o in order]:
            if away == 0:
                start.append(init_factor)
            else:
                pairs = [(r ^ away, r) for r in tree.child_roots(0, depth, 0)]
                start.append(send(rows_in, pairs))
        lefts = {}
        for level in range(2, depth):

            def where(seg, tm, level=level):
                by_rows = seg % 2 == 0 if level == 2 else seg >= 0
                next_rows = tm < half if level == depth - 1 else seg >= 0
                return by_rows, (tm >> level) % 2 == 0, next_rows

            got = [send(c, tree.up(level)) for c in outs]
            if level < depth - 1 or chunks == 1:
                outs, mine, lefts[level] = merge(z, where, got, outs)
            else:
                sent, lefts[level], right = merge_first(z, where, got, outs, 2)
                outs, mine = merge_rest(z, where, sent, lefts[level], right, 2)
        crossed = [send(c, tree.up(depth)) for c in outs]
        final = [part for c in crossed for part in times_chunk(z, in_right_half, c, mine)]
        a, b = tree.child_roots(0, depth, 0)
        halved = send(advance_mean(z, init_mean, mine), [(a, b)])
        onward = advance_mean(z, halved, mine)
        nexts = [(b, size + r) for r in tree.child_roots(1, depth, 0)]
        second = send(onward, nexts[1:]) + send(onward, nexts[:1])
        roots = tree.pairs(lambda odd: [(r, r ^ 1) for r in tree.child_roots(odd, depth, 0)])
        roots = [p for p in roots if p[0] >= size]
        got = [send(c, roots) for c in final]
        left = assemble(z, lambda seg, tm: (seg >= 0, seg % 2 == 1), first, [back])
        halfway = assemble(z, lambda seg, tm: (seg >= 0, seg < 0), crossed)
        got[-1], left, halfway = lax.optimization_barrier((got[-1], left, halfway))

        def beside(seg, tm):
            return tm >= half, tm ^ 1 == tree.root_of(seg % 2, depth - 1, tm // half)

        block = assemble(z, beside, final, got, with_tail=False)

        at_root = assemble(z, lambda seg, tm: (tm >= half, seg < 0), final)
        entries = [init_mean, second]
        for turn in range(2, segs):
            pairs = []
            for h in (0, 1):
                a, b = (tree.root(s % 2, depth - 1, h) for s in (turn - 1, turn))
                pairs.append(((turn - 1) * size + a, turn * size + b))
            gone = advance_mean(z, entries[-1], at_root)
            entries.append(send(gone, pairs))

        same, aside = advance(z, lambda seg, tm: seg == 0, start, at_root, split=True)
        first_roots = tree.child_roots(0, depth, 0)
        moved = pick(
            lambda seg, tm: tm == tree.root_of(0, depth - 1, tm // half),
            same,
            send(aside, [(r, r ^ 1) for r in first_roots]),
        )
        for turn in range(1, segs):
            pairs = [((turn - 1) * size + i, turn * size + i) for i in range(size) if tree.holds(i)]
            if turn == 1:
                arrived = send(same, [(r, size + r) for r in first_roots])
                arrived = arrived + send(aside, [(r, size + (r ^ 1)) for r in first_roots])
            else:
                arrived = send(moved, pairs)

            def where(seg, tm, turn=turn):
                return seg >= turn

            moved = advance(z, where, [arrived], block, moved, turn == segs - 1)

        def down(arrivals, first_seg, last_seg):
            def only(pairs):
                return [p for p in pairs if first_seg <= p[0] // size <= last_seg]

            candidates, cross = arrivals, halfway
            for level in range(depth - 1, 1, -1):

                def where(seg, tm, level=level):
                    if level == depth - 1:
                        index = seg - first_seg
                    else:
                        index = (tm == top_and_other(seg, tm, level + 1)[1]).astype(jnp.int32)
                    return index, tm >= half, (tm >> level) % 2 == 0

                mine_in, other_in = descend(z, where, candidates, lefts[level], cross)
                candidates, cross = [mine_in, send(other_in, only(others(level, 0)))], None
            near = tree.pairs(lambda odd: [(tree.root(odd, 2, g), tree.root(odd, 2, g) ^ 1) for g in range(size >> 2)])
            return [*candidates, send(other_in, only(others(2, 1))), send(mine_in, only(near))]

        candidates = down(entries[:-1], 0, segs - 2) + down(entries[-1:], segs - 1, segs - 1)

        kept, given = moved
        for bit in reversed(bits):
            back_pairs = [(b, a) for a, b in tree.far(bit)]
            came = send(given, back_pairs)

            def where(seg, tm, bit=bit):
                away = tm // 2 ^ tree.root_of(0, depth - 1, tm // half) // 2
                return (away >= bit) & (away < 2 * bit)

            kept = deal(where, kept, came)
            if bit != bits[0]:
                rows = kept.shape[1] // 2
                kept, given = kept[0, :rows], kept[0, rows:]
        ends = kept

        def where(seg, tm):
            top, other = top_and_other(seg, tm, 2)
            index = jnp.where(tm == other, 1, jnp.where(tm == other ^ 1, 2, jnp.where(tm == top, 0, 3)))
            index = index + jnp.where(seg == segs - 1, 4, 0)
            return index, tm % 2 == 1, (seg + tm) % 2 == 1

        return last_steps(z, where, candidates, left, transition, (early, late)), ends

    return per_device


def solution(mesh):
    return jax.shard_map(
        make(mesh),
        mesh=mesh,
        in_specs=(
            P(("seg", "tm"), None, None),
            P(("seg", "tm"), None, None),
            P(("seg", "tm"), None, None),
            P(),
            P("tm", None),
        ),
        out_specs=(P(("seg", "tm"), None, None), P("seg", "tm", None)),
        check_vma=False,
    )
```

```python
import jax
import jax.numpy as jnp
from jax import lax
from jax.experimental import pallas as pl
from jax.experimental.pallas import tpu as pltpu
from jax.sharding import PartitionSpec as P

F32 = jnp.float32
BF16 = jnp.bfloat16
AXES = ("seg", "tm")
GRANT = 10 * 1024 * 1024


def halves(x):
    hi = x.astype(BF16)
    return hi, (x - hi.astype(F32)).astype(BF16)


def dot(a, b):
    return jnp.dot(a, b, preferred_element_type=F32)


def dot3(a_hi, a_lo, b_hi, b_lo):
    return dot(a_hi, b_hi) + (dot(a_hi, b_lo) + dot(a_lo, b_hi))


def few(rows, hi, lo=None):
    r_hi = rows.astype(BF16)
    r_hi32 = r_hi.astype(F32)
    both = jnp.concatenate([r_hi32, rows - r_hi32]).astype(BF16)
    res = dot(both, hi)
    res = res[: rows.shape[0]] + res[rows.shape[0] :]
    return res if lo is None else res + dot(r_hi, lo)


class Sizes:
    def __init__(self, width, series, chunks):
        self.width, self.series, self.chunks = width, series, chunks
        self.part = width // chunks
        self.tall = width + 16 * (-(-series // 16))
        self.buf = width + 8 * (-(-chunks * series // 8))
        self.low = self.tall - width


def put_rows(z, out, body, tail):
    for j in range(z.chunks):
        cols = slice(j * z.part, (j + 1) * z.part)
        out[j * z.part : (j + 1) * z.part, :] = body[:, cols]
        out[z.width + j * z.series : z.width + (j + 1) * z.series, :] = tail[:, cols]


def put_cols(z, out, body, tail):
    out[: z.width, :] = body
    out[z.width : z.width + z.series, :] = tail


def gather_rows(z, bufs, full):
    for k, buf in enumerate(bufs):
        for j in range(z.chunks):
            full[k * z.part : (k + 1) * z.part, j * z.part : (j + 1) * z.part] = buf[j * z.part : (j + 1) * z.part, :]
    for j in range(z.chunks):
        full[z.width : z.width + z.series, j * z.part : (j + 1) * z.part] = bufs[0][
            z.width + j * z.series : z.width + (j + 1) * z.series, :
        ]


def gather_cols(z, bufs, full):
    for k, buf in enumerate(bufs):
        cols = slice(k * z.part, (k + 1) * z.part)
        full[: z.width, cols] = buf[: z.width, :]
        full[z.width : z.width + z.series, cols] = buf[z.width : z.width + z.series, :]


def clear_low(z, full):
    full[z.width :, :] = jnp.zeros((z.low, z.width), F32)


def put_chunks(z, by_rows, outs, full):
    @pl.when(by_rows)
    def _():
        for k, out in enumerate(outs):
            put_rows(z, out, full[k * z.part : (k + 1) * z.part, :], full[z.width : z.width + z.series, :])

    @pl.when(jnp.logical_not(by_rows))
    def _():
        for k, out in enumerate(outs):
            cols = slice(k * z.part, (k + 1) * z.part)
            put_cols(z, out, full[: z.width, cols], full[z.width : z.width + z.series, cols])


def call(kernel, outs, operands, where=None, scratch=(), far=0):
    in_specs = [pl.BlockSpec(memory_space=pltpu.HBM if i < far else pltpu.VMEM) for i in range(len(operands))]
    operands = [pltpu.with_memory_space_constraint(x, pltpu.HBM) if i < far else x for i, x in enumerate(operands)]

    def body(*refs):
        if where is None:
            kernel(*refs)
        else:
            kernel(where(lax.axis_index("seg"), lax.axis_index("tm")), *refs)

    return pl.pallas_call(
        body,
        out_shape=outs,
        in_specs=in_specs,
        out_specs=jax.tree.map(lambda _: pl.BlockSpec(memory_space=pltpu.VMEM), outs),
        scratch_shapes=list(scratch),
        compiler_params=pltpu.CompilerParams(vmem_limit_bytes=GRANT),
    )(*operands)


def shape(rows, cols, dtype=F32):
    return jax.ShapeDtypeStruct((rows, cols), dtype)


def gather(z, by_rows, bufs, full):
    @pl.when(by_rows)
    def _():
        gather_rows(z, bufs, full)

    @pl.when(jnp.logical_not(by_rows))
    def _():
        gather_cols(z, bufs, full)


def map_shapes(z):
    return [shape(z.tall, z.width, BF16), shape(z.tall, z.width, BF16), shape(z.series, z.width)]


def local_map(z, where, transition, gain, observed, sender):
    steps = transition.shape[0]
    count = z.chunks if sender else 4

    def kernel(flag, *refs):
        by_rows, active = flag
        pl.when(active)(lambda: run(by_rows, *refs))

    def run(by_rows, t_hbm, g_hbm, o_hbm, *rest):
        outs, drive, t, g, o, sems = rest[:count], *rest[count : count + 5]
        whole = rest[-1] if sender else outs[0]
        copies = [
            pltpu.make_async_copy(t_hbm, t, sems.at[0]),
            pltpu.make_async_copy(g_hbm, g, sems.at[1]),
            pltpu.make_async_copy(o_hbm, o, sems.at[2]),
        ]
        for copy in copies:
            copy.start()
        copies[0].wait()
        body = t[0]
        for i in range(1, steps):
            if i == 1:
                body = dot(body, t[i])
            else:
                b_hi, b_lo = halves(body)
                body = dot(b_hi, t[i]) + dot(b_lo, t[i])
        clear_low(z, whole)
        whole[: z.width, :] = body.astype(F32)
        copies[1].wait()
        copies[2].wait()
        drives = [dot(o[i], g[i]) for i in range(steps)]
        low = drives[0]
        for i in range(steps):
            drive[i] = drives[i]
            if i:
                l_hi, l_lo = halves(low)
                low = dot(l_hi, t[i]) + dot(l_lo, t[i]) + drives[i]
        whole[z.width : z.width + z.series, :] = low
        if sender:
            put_chunks(z, by_rows, outs, whole)
        else:
            _, hi, lo, tail = outs
            tail[...] = low
            hi[...], lo[...] = halves(whole[...])

    shapes = [shape(z.buf, z.part)] * z.chunks if sender else [shape(z.tall, z.width), *map_shapes(z)]
    res = call(
        kernel,
        shapes + [jax.ShapeDtypeStruct((steps, z.series, z.width), F32)],
        [transition, gain, observed],
        where,
        scratch=[
            pltpu.VMEM(transition.shape, transition.dtype),
            pltpu.VMEM(gain.shape, gain.dtype),
            pltpu.VMEM(observed.shape, observed.dtype),
            pltpu.SemaphoreType.DMA((3,)),
        ]
        + ([pltpu.VMEM((z.tall, z.width), F32)] if sender else []),
        far=3,
    )
    return (res[:-1], res[-1]) if sender else (res[0], tuple(res[1:4]), res[-1])


def quarter(z, ref, k):
    return ref.at[pl.ds(k * z.buf, z.buf)]


def split_parts(z, refs):
    return [quarter(z, ref, k) for ref in refs for k in range(ref.shape[0] // z.buf)]


def times_chunk(z, where, chunk, own):
    count = chunk.shape[0] // z.buf
    span = count * z.part

    def kernel(by_rows, got, own_hi, own_lo, own_tail, res_out, left, right):
        outs = split_parts(z, [res_out])
        gots = split_parts(z, [got])

        @pl.when(by_rows)
        def _():
            left[span:, :] = jnp.zeros((left.shape[0] - span, z.width), F32)
            for j in range(z.chunks):
                cols = slice(j * z.part, (j + 1) * z.part)
                for q, part in enumerate(gots):
                    left[q * z.part : (q + 1) * z.part, cols] = part[j * z.part : (j + 1) * z.part, :]
                left[span : span + z.series, cols] = gots[0][z.width + j * z.series : z.width + (j + 1) * z.series, :]
            l_hi, l_lo = halves(left[...])
            res = dot3(l_hi, l_lo, own_hi[: z.width, :], own_lo[: z.width, :])
            for q, out in enumerate(outs):
                put_rows(z, out, res[q * z.part : (q + 1) * z.part], res[span : span + z.series] + own_tail[...])

        @pl.when(jnp.logical_not(by_rows))
        def _():
            for q, part in enumerate(gots):
                right[:, q * z.part : (q + 1) * z.part] = part[: z.width + z.series, :]
            r_hi, r_lo = halves(right[: z.width, :])
            res = dot3(own_hi[...], own_lo[...], r_hi, r_lo)
            low = res[z.width : z.width + z.series] + right[z.width : z.width + z.series, :]
            for q, out in enumerate(outs):
                cols = slice(q * z.part, (q + 1) * z.part)
                out[z.width :, :] = jnp.zeros((z.buf - z.width, z.part), F32)
                put_cols(z, out, res[: z.width, cols], low[:, cols])

    return call(
        kernel,
        [shape(count * z.buf, z.part)],
        [chunk, *own],
        where,
        scratch=[pltpu.VMEM((span + z.low, z.width), F32), pltpu.VMEM((z.width + z.series, span), F32)],
    )


def merge(z, where, got, own):
    sent = z.chunks

    def kernel(flag, *refs):
        by_rows, got_left, next_rows = flag
        n = z.chunks
        gots, owns = refs[:n], refs[n : 2 * n]
        outs = split_parts(z, refs[2 * n : 2 * n + sent])
        hi, lo, tail, left_hi, left_lo, left_tail = refs[2 * n + sent : 2 * n + sent + 6]
        a, b, c = refs[2 * n + sent + 6 :]
        clear_low(z, a)
        clear_low(z, b)

        @pl.when(got_left)
        def _():
            gather(z, by_rows, gots, a)
            gather(z, by_rows, owns, b)

        @pl.when(jnp.logical_not(got_left))
        def _():
            gather(z, by_rows, owns, a)
            gather(z, by_rows, gots, b)

        left_hi[...], left_lo[...] = halves(a[...])
        left_tail[...] = a[z.width : z.width + z.series, :]
        r_hi, r_lo = halves(b[: z.width, :])
        c[...] = dot3(left_hi[...], left_lo[...], r_hi, r_lo)
        c[z.width : z.width + z.series, :] = c[z.width : z.width + z.series, :] + b[z.width : z.width + z.series, :]
        put_chunks(z, next_rows, outs, c)
        hi[...], lo[...] = halves(c[...])
        tail[...] = c[z.width : z.width + z.series, :]

    res = call(
        kernel,
        [shape(z.chunks // sent * z.buf, z.part)] * sent + map_shapes(z) * 2,
        list(got) + list(own),
        where,
        scratch=[pltpu.VMEM((z.tall, z.width), F32)] * 3,
    )
    return res[:sent], tuple(res[sent : sent + 3]), tuple(res[sent + 3 :])


def merge_first(z, where, got, own, count):
    span = z.width // count
    n = z.chunks

    def kernel(flag, *refs):
        by_rows, got_left, next_rows = flag
        gots, owns = refs[:n], refs[n : 2 * n]
        out, left_hi, left_lo, left_tail, right_hi, right_lo, right_tail, a, b, c = refs[2 * n :]
        outs = split_parts(z, [out])
        clear_low(z, a)
        clear_low(z, b)

        @pl.when(got_left)
        def _():
            gather(z, by_rows, gots, a)
            gather(z, by_rows, owns, b)

        @pl.when(jnp.logical_not(got_left))
        def _():
            gather(z, by_rows, owns, a)
            gather(z, by_rows, gots, b)

        left_hi[...], left_lo[...] = halves(a[...])
        left_tail[...] = a[z.width : z.width + z.series, :]
        right_hi[...], right_lo[...] = halves(b[...])
        tail = b[z.width : z.width + z.series, :]
        right_tail[...] = tail

        @pl.when(next_rows)
        def _():
            c[:span, :] = a[:span, :]
            c[span : span + z.low, :] = a[z.width :, :]
            c_hi, c_lo = halves(c[: span + z.low, :])
            res = dot3(c_hi, c_lo, right_hi[: z.width, :], right_lo[: z.width, :])
            for q, part in enumerate(outs):
                put_rows(z, part, res[q * z.part : (q + 1) * z.part], res[span : span + z.series] + tail)

        @pl.when(jnp.logical_not(next_rows))
        def _():
            res = dot3(left_hi[...], left_lo[...], right_hi[: z.width, :span], right_lo[: z.width, :span])
            for q, part in enumerate(outs):
                cols = slice(q * z.part, (q + 1) * z.part)
                put_cols(z, part, res[: z.width, cols], res[z.width : z.width + z.series, cols] + tail[:, cols])

    res = call(
        kernel,
        [shape(z.chunks // count * z.buf, z.part)] + map_shapes(z) * 2,
        list(got) + list(own),
        where,
        scratch=[pltpu.VMEM((z.tall, z.width), F32)] * 3,
    )
    return res[0], tuple(res[1:4]), tuple(res[4:7])


def merge_rest(z, where, sent, left, right, count):
    span = z.width // count

    def kernel(flag, *refs):
        next_rows = flag[2]
        done, left_hi, left_lo, _, right_hi, right_lo, right_tail = refs[:7]
        outs = split_parts(z, refs[7 : 6 + count])
        hi, lo, tail, c = refs[6 + count :]
        gather(z, next_rows, split_parts(z, [done]), c)

        @pl.when(next_rows)
        def _():
            c[span:, :] = dot3(left_hi[span:, :], left_lo[span:, :], right_hi[: z.width, :], right_lo[: z.width, :])
            low = c[z.width : z.width + z.series, :] + right_tail[...]
            c[z.width : z.width + z.series, :] = low
            for q, part in enumerate(outs):
                at = span + q * z.part
                put_rows(z, part, c[at : at + z.part, :], low)

        @pl.when(jnp.logical_not(next_rows))
        def _():
            c[z.width + z.series :, :span] = jnp.zeros((z.low - z.series, span), F32)
            c[:, span:] = dot3(left_hi[...], left_lo[...], right_hi[: z.width, span:], right_lo[: z.width, span:])
            low = c[z.width : z.width + z.series, span:] + right_tail[:, span:]
            c[z.width : z.width + z.series, span:] = low
            for q, part in enumerate(outs):
                cols = slice(span + q * z.part, span + (q + 1) * z.part)
                put_cols(z, part, c[: z.width, cols], low[:, q * z.part : (q + 1) * z.part])

        hi[...], lo[...] = halves(c[...])
        tail[...] = c[z.width : z.width + z.series, :]

    res = call(
        kernel,
        [shape(z.chunks // count * z.buf, z.part)] * (count - 1) + map_shapes(z),
        [sent, *left, *right],
        where,
        scratch=[pltpu.VMEM((z.tall, z.width), F32)],
    )
    return [sent, *res[: count - 1]], tuple(res[count - 1 :])


def assemble(z, where, chunks, others=None, with_tail=True):
    extra = [] if others is None else list(others)

    def kernel(flag, *refs):
        by_rows, swap = flag
        n = len(chunks)
        bufs, rest = split_parts(z, refs[:n]), refs[n : n + len(extra)]
        hi, lo, *tail, full = refs[n + len(extra) :]
        clear_low(z, full)
        if not extra:
            gather(z, by_rows, bufs, full)
        else:

            @pl.when(jnp.logical_not(swap))
            def _():
                gather(z, by_rows, bufs, full)

            @pl.when(swap)
            def _():
                if rest[0].shape[0] == z.tall:
                    full[...] = rest[0][...]
                else:
                    gather(z, by_rows, split_parts(z, rest), full)

        hi[...], lo[...] = halves(full[...])
        if with_tail:
            tail[0][...] = full[z.width : z.width + z.series, :]

    return call(
        kernel,
        map_shapes(z) if with_tail else map_shapes(z)[:2],
        list(chunks) + extra,
        where,
        scratch=[pltpu.VMEM((z.tall, z.width), F32)],
    )


def padded(series):
    return 8 * (-(-series // 8))


def advance(z, where, parts, block, before=None, split=False):
    rows = sum(p.shape[0] for p in parts)
    operands = list(parts) + list(block[:2]) + ([] if before is None else [before])
    m = len(parts)

    def kernel(active, *refs):
        given, (hi, lo), outs = refs[:m], refs[m : m + 2], refs[len(operands) :]

        def put(value):
            for i, out in enumerate(outs):
                out[...] = value[i * out.shape[0] : (i + 1) * out.shape[0]]

        def run():
            state = given[0][...] if m == 1 else jnp.concatenate([g[...] for g in given])
            put(few(state, hi[: z.width, :], lo[: z.width, :]))

        pl.when(active)(run)
        if before is not None:

            @pl.when(jnp.logical_not(active))
            def _():
                put(refs[m + 2][...])

    outs = [shape(rows // 2, z.width)] * 2 if split else [shape(rows, z.width)]
    res = call(kernel, outs, operands, where)
    return res if split else res[0]


def pick_halves(where, whole, parts):
    rows = parts[0].shape[0]

    def kernel(flag, a, b, c, first, second):
        @pl.when(flag)
        def _():
            first[...] = a[:rows]
            second[...] = a[rows:]

        @pl.when(jnp.logical_not(flag))
        def _():
            first[...] = b[...]
            second[...] = c[...]

    return call(kernel, [shape(*p.shape) for p in parts], [whole, *parts], where)


def advance_mean(z, mean, block):
    low = padded(z.series)

    def kernel(given, hi, lo, tail, out):
        now = given[...]
        if given.shape[0] < low:
            now = jnp.concatenate([now, jnp.zeros((low - given.shape[0], z.width), F32)])
        out[...] = few(now, hi[: z.width, :], lo[: z.width, :])
        out[: z.series, :] = out[: z.series, :] + tail[...]

    return call(kernel, shape(low, z.width), [mean, *block])


def deal(where, kept, got):
    def kernel(received, a, b, out):
        @pl.when(received)
        def _():
            out[0] = b[...]

        @pl.when(jnp.logical_not(received))
        def _():
            out[0] = a[...]

    return call(kernel, jax.ShapeDtypeStruct((1, *kept.shape), F32), [kept, got], where)


def load_choice(z, index, refs, into):
    for i, ref in enumerate(refs):

        @pl.when(index == i)
        def _():
            if ref.shape[0] == z.series:
                into[...] = jnp.zeros(into.shape, F32)
                into[: z.series, :] = ref[...]
            else:
                into[...] = ref[ref.shape[0] - into.shape[0] :, :]


def descend(z, where, candidates, left, cross=None):
    low = padded(z.series)
    m = len(candidates)
    maps = list(left) + ([] if cross is None else list(cross))

    def kernel(flag, *refs):
        pl.when((flag[0] >= 0) & (flag[0] < m))(lambda: run(flag, *refs))

    def run(flag, *refs):
        index, through, in_right = flag
        hi, lo, tail = refs[m : m + 3]
        mine, other, now = refs[m + len(maps) :]
        load_choice(z, index, refs[:m], now)
        if cross is not None:

            @pl.when(through)
            def _():
                c_hi, c_lo, c_tail = refs[m + 3 : m + 6]
                now[...] = few(now[...], c_hi[: z.width, :], c_lo[: z.width, :])
                now[: z.series, :] = now[: z.series, :] + c_tail[...]

        beyond = few(now[...], hi[: z.width, :], lo[: z.width, :])

        @pl.when(in_right)
        def _():
            mine[...] = beyond
            mine[: z.series, :] = mine[: z.series, :] + tail[...]
            other[...] = now[...]

        @pl.when(jnp.logical_not(in_right))
        def _():
            other[...] = beyond
            other[: z.series, :] = other[: z.series, :] + tail[...]
            mine[...] = now[...]

    return call(
        kernel, [shape(low, z.width)] * 2, [*candidates, *maps], where, scratch=[pltpu.VMEM((low, z.width), F32)]
    )


def last_steps(z, where, candidates, left, transition, drives):
    steps = transition.shape[0]
    m = len(candidates)
    low = padded(z.series)

    def kernel(flag, *refs):
        index, through, second = flag
        hi, lo, tail, t, d0, d1, out, now = refs[m:]
        load_choice(z, index, refs[:m], now)

        @pl.when(through)
        def _():
            now[...] = few(now[...], hi[: z.width, :], lo[: z.width, :])
            now[: z.series, :] = now[: z.series, :] + tail[...]

        for i in range(steps):
            now[...] = few(now[...], t[i])
            now[: z.series, :] = now[: z.series, :] + jnp.where(second, d1[i], d0[i])
            out[i] = now[: z.series, :]

    return call(
        kernel,
        jax.ShapeDtypeStruct((steps, z.series, z.width), F32),
        [*candidates, *left, transition, *drives],
        where,
        scratch=[pltpu.VMEM((low, z.width), F32)],
    )


class Tree:
    def __init__(self, segs, size):
        self.segs, self.size = segs, size
        self.depth = size.bit_length() - 1
        if size != 1 << self.depth or self.depth < 3:
            raise ValueError("tm size")

    def root(self, odd, level, group):
        if level == 1:
            return 2 * group + (0 if odd else 1)
        return self.root(odd, level - 1, 2 * group + (1 - group % 2))

    def pairs(self, per_parity):
        return [
            (s * self.size + a, s * self.size + b) for s in range(self.segs) for a, b in per_parity(s % 2)
        ]

    def child_roots(self, odd, level, group):
        return self.root(odd, level - 1, 2 * group), self.root(odd, level - 1, 2 * group + 1)

    def up(self, level):
        def of(odd):
            if level == 1:
                return [(i, i ^ 1) for i in range(self.size) if i % 2 == (1 if odd else 0)]
            found = []
            for g in range(self.size >> level):
                a, b = self.child_roots(odd, level, g)
                if level == self.depth:
                    found += [(a, b), (b, a)]
                else:
                    found.append((a, b) if g % 2 == 0 else (b, a))
            return found

        return self.pairs(of)

    def far(self, bit, seg=None):
        found = []
        for s in range(self.segs) if seg is None else [seg]:
            for i in range(self.size):
                away = i // 2 ^ self.root(0, self.depth - 1, 2 * i // self.size) // 2
                if bit <= away < 2 * bit:
                    found.append((s * self.size + i, s * self.size + (i ^ 2 * bit)))
        return found

    def holds(self, i):
        return i // 2 == self.root(0, self.depth - 1, 2 * i // self.size) // 2

    def root_of(self, odd, level, group):
        for _ in range(level - 1):
            group = 2 * group + 1 - group % 2
        return 2 * group + 1 - odd


def tied(x, after):
    return lax.optimization_barrier((x, after))[0]


def make(mesh):
    segs, size = mesh.shape["seg"], mesh.shape["tm"]
    tree = Tree(segs, size)
    depth = tree.depth
    half = size // 2

    def send(x, pairs):
        return lax.ppermute(x, AXES, pairs)

    def others(level, flip):
        def of(odd):
            found = []
            for g in range(size >> level):
                root = tree.root(odd, level, g)
                a, b = tree.child_roots(odd, level, g)
                found.append((root, (a if root == b else b) ^ flip))
            return found

        return tree.pairs(of)

    def top_and_other(seg, tm, level):
        odd, group = seg % 2, tm >> level
        top = tree.root_of(odd, level, group)
        a, b = (tree.root_of(odd, level - 1, 2 * group + i) for i in (0, 1))
        return top, a + b - top

    def per_device(transition, obs_gain, observed, init_mean, init_factor):
        width, series = transition.shape[1], observed.shape[1]
        chunks = next(n for n in (4, 2, 1) if width % (n * 128) == 0 or n == 1)
        z = Sizes(width, series, chunks)

        def is_even(seg, tm):
            return seg % 2 == 0

        def in_right_half(seg, tm):
            return tm >= half

        def sends(seg, tm):
            return seg % 2 == 0, (seg + tm) % 2 == 0

        def receives(seg, tm):
            return seg % 2 == 0, (seg + tm) % 2 == 1

        def one_chunk(c):
            return times_chunk(z, is_even, c, own_map)[0]

        own, early = local_map(z, sends, transition, obs_gain, observed, True)
        first = [send(c, tree.up(1)) for c in own]
        whole, own_map, late = local_map(z, receives, transition, obs_gain, observed, False)
        outs = [one_chunk(c) for c in first]
        back = send(tied(whole, outs), tree.pairs(lambda odd: [(i, i + 1) for i in range(0, size, 2)] if odd else []))
        order, bits = [0], [1 << i for i in range(depth - 3, -1, -1)]
        for bit in bits:
            order += [o ^ bit for o in order]
        rows_in = tied(init_factor, outs)
        start = []
        for away in [2 * o for o in order] + [2 * o ^ 1 for o in order]:
            if away == 0:
                start.append(init_factor)
            else:
                pairs = [(r ^ away, r) for r in tree.child_roots(0, depth, 0)]
                start.append(send(rows_in, pairs))
        lefts = {}
        for level in range(2, depth):

            def where(seg, tm, level=level):
                by_rows = seg % 2 == 0 if level == 2 else seg >= 0
                next_rows = tm < half if level == depth - 1 else seg >= 0
                return by_rows, (tm >> level) % 2 == 0, next_rows

            got = [send(c, tree.up(level)) for c in outs]
            if level < depth - 1 or chunks == 1:
                outs, mine, lefts[level] = merge(z, where, got, outs)
            else:
                sent, lefts[level], right = merge_first(z, where, got, outs, 2)
                outs, mine = merge_rest(z, where, sent, lefts[level], right, 2)
        crossed = [send(c, tree.up(depth)) for c in outs]
        final = [part for c in crossed for part in times_chunk(z, in_right_half, c, mine)]
        a, b = tree.child_roots(0, depth, 0)
        halved = send(advance_mean(z, init_mean, mine), [(a, b)])
        onward = advance_mean(z, halved, mine)
        nexts = [(b, size + r) for r in tree.child_roots(1, depth, 0)]
        second = send(onward, nexts[1:]) + send(onward, nexts[:1])
        roots = tree.pairs(lambda odd: [(r, r ^ 1) for r in tree.child_roots(odd, depth, 0)])
        got = [send(c, [p for p in roots if p[0] // size == 1]) for c in final]
        rest = [send(c, [p for p in roots if p[0] // size > 1]) for c in final]
        left = assemble(z, lambda seg, tm: (seg >= 0, seg % 2 == 1), first, [back])
        halfway = assemble(z, lambda seg, tm: (seg >= 0, seg < 0), crossed)
        rest[-1], left, halfway = lax.optimization_barrier((rest[-1], left, halfway))

        def beside(seg, tm):
            return tm >= half, tm ^ 1 == tree.root_of(seg % 2, depth - 1, tm // half)

        block = assemble(z, beside, final, got, with_tail=False)
        later = assemble(z, beside, final, rest, with_tail=False)

        at_root = assemble(z, lambda seg, tm: (tm >= half, seg < 0), final)
        entries = [init_mean, second]
        for turn in range(2, segs):
            pairs = []
            for h in (0, 1):
                a, b = (tree.root(s % 2, depth - 1, h) for s in (turn - 1, turn))
                pairs.append(((turn - 1) * size + a, turn * size + b))
            gone = advance_mean(z, entries[-1], at_root)
            entries.append(send(gone, pairs))

        same, aside = advance(z, lambda seg, tm: seg == 0, start, at_root, split=True)
        first_roots = tree.child_roots(0, depth, 0)
        beside_first = send(aside, [(r, r ^ 1) for r in first_roots])
        moved = same
        for turn in range(1, segs):
            pairs = [((turn - 1) * size + i, turn * size + i) for i in range(size) if tree.holds(i)]
            if turn == 1:
                arrived = send(same, [(r, size + r) for r in first_roots])
                arrived = arrived + send(aside, [(r, size + (r ^ 1)) for r in first_roots])
            else:
                arrived = send(moved, pairs)

            def where(seg, tm, turn=turn):
                return seg >= turn

            moved = advance(z, where, [arrived], block if turn == 1 else later, moved, turn == segs - 1)

        def down(arrivals, first_seg, last_seg):
            def only(pairs):
                return [p for p in pairs if first_seg <= p[0] // size <= last_seg]

            candidates, cross = arrivals, halfway
            for level in range(depth - 1, 1, -1):

                def where(seg, tm, level=level):
                    if level == depth - 1:
                        index = seg - first_seg
                    else:
                        index = (tm == top_and_other(seg, tm, level + 1)[1]).astype(jnp.int32)
                    return index, tm >= half, (tm >> level) % 2 == 0

                mine_in, other_in = descend(z, where, candidates, lefts[level], cross)
                candidates, cross = [mine_in, send(other_in, only(others(level, 0)))], None
            near = tree.pairs(lambda odd: [(tree.root(odd, 2, g), tree.root(odd, 2, g) ^ 1) for g in range(size >> 2)])
            return [*candidates, send(other_in, only(others(2, 1))), send(mine_in, only(near))]

        candidates = down(entries[:-1], 0, segs - 2) + down(entries[-1:], segs - 1, segs - 1)

        kept, given = pick_halves(
            lambda seg, tm: (seg == 0) & (tm == tree.root_of(0, depth - 1, tm // half) ^ 1), beside_first, moved
        )
        for bit in reversed(bits):
            back_pairs = [(b, a) for a, b in tree.far(bit)]
            came = send(given, back_pairs)

            def where(seg, tm, bit=bit):
                away = tm // 2 ^ tree.root_of(0, depth - 1, tm // half) // 2
                return (away >= bit) & (away < 2 * bit)

            kept = deal(where, kept, came)
            if bit != bits[0]:
                rows = kept.shape[1] // 2
                kept, given = kept[0, :rows], kept[0, rows:]
        ends = kept

        def where(seg, tm):
            top, other = top_and_other(seg, tm, 2)
            index = jnp.where(tm == other, 1, jnp.where(tm == other ^ 1, 2, jnp.where(tm == top, 0, 3)))
            index = index + jnp.where(seg == segs - 1, 4, 0)
            return index, tm % 2 == 1, (seg + tm) % 2 == 1

        return last_steps(z, where, candidates, left, transition, (early, late)), ends

    return per_device


def solution(mesh):
    return jax.shard_map(
        make(mesh),
        mesh=mesh,
        in_specs=(
            P(("seg", "tm"), None, None),
            P(("seg", "tm"), None, None),
            P(("seg", "tm"), None, None),
            P(),
            P("tm", None),
        ),
        out_specs=(P(("seg", "tm"), None, None), P("seg", "tm", None)),
        check_vma=False,
    )
```
